32 devices in a mesh: ctx: 8 (over z, core), fsdp: 4 (over y, x).
Axes of the slice: x: 2, y: 2, z: 4, core: 2. Of those that a mesh axis runs over, the one named last changes fastest.
Arguments:
- inputs: float32 [4, 16, 64, 1024], P('fsdp', 'ctx'), may hold values from -6 to 6
- block_order: int32 [16], replicated, may hold values from 0 to 15, as said below
- w_qkv: bfloat16 [1, 1024, 3072], P(None, 'fsdp'), may hold values from -0.1875 to 0.1875
- w_out: bfloat16 [1, 1024, 1024], P(None, 'fsdp'), may hold values from -1.5 to 1.5
- w_up: bfloat16 [1, 1024, 4096], P(None, 'fsdp'), may hold values from -0.1875 to 0.1875
- w_down: bfloat16 [1, 4096, 1024], P(None, 'fsdp'), may hold values from -0.09375 to 0.09375
- norm_gains: bfloat16 [1, 2, 1024], P(None, None, 'fsdp'), may hold values from 0.099609375 to 1.8984375
- biases: bfloat16 [1, 6, 1024], P(None, None, 'fsdp'), may hold values from -2.390625 to 2.390625
- up_bias: bfloat16 [1, 4096], P(None, 'fsdp'), may hold values from -2.390625 to 2.390625
- out_grad: float32 [4, 16, 64, 1024], P('fsdp', 'ctx'), may hold values from -6 to 6
Outputs:
- outputs: float32 [4, 16, 64, 1024], P('fsdp', 'ctx')
- input_grad: float32 [4, 16, 64, 1024], P('fsdp', 'ctx')
- g_qkv: float32 [1, 1024, 3072], P(None, ('ctx', 'fsdp'))
- g_out: float32 [1, 1024, 1024], P(None, ('ctx', 'fsdp'))
- g_up: float32 [1, 1024, 4096], P(None, ('ctx', 'fsdp'))
- g_down: float32 [1, 4096, 1024], P(None, ('ctx', 'fsdp'))
- g_gains: float32 [1, 2, 1024], P(None, None, ('ctx', 'fsdp'))
- g_biases: float32 [1, 6, 1024], P(None, None, ('ctx', 'fsdp'))
- g_up_bias: float32 [1, 4096], P(None, ('ctx', 'fsdp'))
The draws below stay inside these ranges and needn't reach their ends.
Inputs may be any that keep to these rules, and one draw needn't show every extreme that they name: `block_order`: every block number appears once; slots 2c and 2c + 1 hold a pair b and 15 - b, in either order.
All inputs are finite; a program needn't handle non-finite values.
Results may differ from the reference program's by a relative error of at most 0.013.
Values may be sent and summed in bfloat16 or wider, within the bound.
No kernel may reach another device: no remote copies, remote signals or barrier semaphores. Data moves between devices by JAX's collectives and lax.ppermute only.
A program may use at most 192 MiB of HBM per device.

```python
import jax
import jax.numpy as jnp
from jax import lax

D = 1024
HEADS = 16
HD = 64
FF = 4096
BLK = 64
LAYERS = 1
BLOCKS = 16
LENGTH = 1024
SEQS = 4


def draw_block_order(key, part):
    half = BLOCKS // 2
    first_key, second_key = jax.random.split(jax.random.fold_in(key, 11))
    pairs = jax.random.permutation(first_key, half).astype(jnp.int32)
    flips = jax.random.randint(second_key, (half,), 0, 2)
    mirror = (BLOCKS - 1 - pairs).astype(jnp.int32)
    first = jnp.where(flips == 1, mirror, pairs)
    second = jnp.where(flips == 1, pairs, mirror)
    return jnp.stack([first, second], axis=1).reshape(BLOCKS).astype(jnp.int32)


def level_of(key, dims, pieces, smallest, top_value):
    def one(axis_at, blocks):
        draws = jax.random.uniform(jax.random.fold_in(jax.random.fold_in(key, 6), axis_at), (blocks,), jnp.float32, smallest / len(pieces), top_value / len(pieces))
        return jnp.repeat(jnp.exp(draws), dims[axis_at] // blocks).reshape((-1,) + (1,) * (len(dims) - axis_at - 1))

    level = one(*pieces[0])
    for cut in pieces[1:]:
        level = level * one(*cut)
    return level


def normal_values(key, dims, spread, reach, cuts=(), kind=jnp.bfloat16):
    values = spread * jax.random.normal(key, dims, jnp.float32)
    if cuts:
        values = values * level_of(key, dims, cuts, -0.22, 0.18)
    return jnp.clip(values, -reach, reach).astype(kind)


def setup_inputs(seed: int = 0) -> dict:
    key_of = jax.random.split(jax.random.key(seed), 11)
    inputs = normal_values(key_of[0], (SEQS, BLOCKS, BLK, D), 1.0, 6.0, ((0, 4), (1, 8)), jnp.float32)
    block_order = draw_block_order(jax.random.fold_in(key_of[10], 71), 0)
    w_qkv = normal_values(key_of[2], (LAYERS, D, 3 * D), D ** -0.5, 0.1875, ((1, 4),))
    w_out = normal_values(key_of[3], (LAYERS, D, D), (D // 64) ** -0.5, 1.5, ((1, 4),))
    w_up = normal_values(key_of[4], (LAYERS, D, FF), D ** -0.5, 0.1875, ((1, 4),))
    w_down = normal_values(key_of[5], (LAYERS, FF, D), FF ** -0.5, 0.09375, ((1, 4),))
    norm_gains = jnp.clip(1.0 + 0.18 * jax.random.normal(key_of[6], (LAYERS, 2, D), jnp.float32), 0.099609375, 1.8984375).astype(jnp.bfloat16)
    biases = normal_values(key_of[7], (LAYERS, 6, D), 0.4, 2.390625, ((2, 4),))
    up_bias = normal_values(key_of[8], (LAYERS, FF), 0.4, 2.390625, ((1, 4),))
    out_grad = normal_values(key_of[9], (SEQS, BLOCKS, BLK, D), 1.0, 6.0, ((0, 4), (1, 8)), jnp.float32)
    return dict(inputs=inputs, block_order=block_order, w_qkv=w_qkv, w_out=w_out, w_up=w_up, w_down=w_down, norm_gains=norm_gains, biases=biases, up_bias=up_bias, out_grad=out_grad)


EPS = 1e-05
SCALE = 0.125
GELU_C = 0.7978845608028654

def normalize(x):
    centred = x - lax.optimization_barrier(jnp.mean(x, axis=1, keepdims=True))
    inv = lax.rsqrt(lax.optimization_barrier(jnp.mean(centred * centred, axis=1, keepdims=True)) + EPS)
    return (centred * inv, inv)

def norm_back(grad, normed, inv):
    return inv * (grad - lax.optimization_barrier(jnp.mean(grad, axis=1, keepdims=True)) - normed * lax.optimization_barrier(jnp.mean(grad * normed, axis=1, keepdims=True)))

def gelu_parts(u):
    inner = GELU_C * (u + 0.044715 * u * u * u)
    tanhed = jnp.tanh(inner)
    value = 0.5 * u * (1.0 + tanhed)
    slope = 0.5 * (1.0 + tanhed) + 0.5 * u * (1.0 - tanhed * tanhed) * GELU_C * (1.0 + 3.0 * 0.044715 * u * u)
    return (value, slope)

def outer(left, right):
    return lax.dot_general(left, right, (((0,), (0,)), ((), ())), preferred_element_type=jnp.float32)

def through(left, weight):
    return lax.dot_general(left, weight, (((1,), (1,)), ((), ())), preferred_element_type=jnp.float32)

def head_forward(query, keys, values, qpos, kpos):
    allowed = kpos[None, :] <= qpos[:, None]
    scores = jnp.where(allowed, through(query, keys), -1e+30)
    top = lax.optimization_barrier(jnp.max(scores, axis=1, keepdims=True))
    lse = top + jnp.log(lax.optimization_barrier(jnp.sum(jnp.exp(scores - top), axis=1, keepdims=True)))
    probs = jnp.exp(scores - lse).astype(jnp.bfloat16)
    attended = jnp.dot(probs, values, preferred_element_type=jnp.float32).astype(jnp.bfloat16)
    return (attended, lse[:, 0])

def head_backward(query, keys, values, attended, d_att, lse, qpos, kpos):
    allowed = kpos[None, :] <= qpos[:, None]
    scores = through(query, keys)
    probs = jnp.where(allowed, jnp.exp(jnp.where(allowed, scores, 0.0) - lse[:, None]), 0.0)
    delta = lax.optimization_barrier(jnp.sum(d_att.astype(jnp.float32) * attended.astype(jnp.float32), axis=1, keepdims=True))
    d_probs = through(d_att, values)
    d_scores = (probs * (d_probs - delta)).astype(jnp.bfloat16)
    d_query = jnp.dot(d_scores, keys, preferred_element_type=jnp.float32)
    d_keys = outer(d_scores, query)
    d_values = outer(probs.astype(jnp.bfloat16), d_att)
    return (d_query, d_keys, d_values)

def before_attention(x, params):
    w_qkv, w_out, w_up, w_down, gains, biases, up_bias = params
    width = x.shape[1]
    gain = gains.astype(jnp.float32)
    shift = biases.astype(jnp.float32)
    normed, inv = normalize(x)
    a_one = (normed * gain[0] + shift[0]).astype(jnp.bfloat16)
    proj = jnp.dot(a_one, w_qkv, preferred_element_type=jnp.float32)
    query = ((proj[:, :width] + shift[1]) * SCALE).astype(jnp.bfloat16)
    keys = proj[:, width:2 * width].astype(jnp.bfloat16)
    values = (proj[:, 2 * width:] + shift[2]).astype(jnp.bfloat16)
    return ((normed, inv, a_one), query, keys, values)

def after_attention(x, attended, params):
    w_qkv, w_out, w_up, w_down, gains, biases, up_bias = params
    gain = gains.astype(jnp.float32)
    shift = biases.astype(jnp.float32)
    mid = x + jnp.dot(attended, w_out, preferred_element_type=jnp.float32) + shift[3]
    normed, inv = normalize(mid)
    a_two = (normed * gain[1] + shift[4]).astype(jnp.bfloat16)
    hidden = jnp.dot(a_two, w_up, preferred_element_type=jnp.float32) + up_bias.astype(jnp.float32)
    value, slope = gelu_parts(hidden)
    gelled = value.astype(jnp.bfloat16)
    result = mid + jnp.dot(gelled, w_down, preferred_element_type=jnp.float32) + shift[5]
    return (result, (normed, inv, a_two, slope, gelled))

def mlp_backward(d_result, attended, late, params):
    w_qkv, w_out, w_up, w_down, gains, biases, up_bias = params
    gain = gains.astype(jnp.float32)
    normed, inv, a_two, slope, gelled = late
    d_low = d_result.astype(jnp.bfloat16)
    g_down = outer(gelled, d_low)
    d_pre = through(d_low, w_down) * slope
    d_hidden = d_pre.astype(jnp.bfloat16)
    g_up = outer(a_two, d_hidden)
    d_a_two = through(d_hidden, w_up)
    d_mid = d_result + norm_back(d_a_two * gain[1], normed, inv)
    d_low_mid = d_mid.astype(jnp.bfloat16)
    g_out = outer(attended, d_low_mid)
    d_att = through(d_low_mid, w_out).astype(jnp.bfloat16)
    sums = (lax.optimization_barrier(jnp.sum(d_a_two * normed, axis=0)), lax.optimization_barrier(jnp.sum(d_a_two, axis=0)), lax.optimization_barrier(jnp.sum(d_mid, axis=0)), lax.optimization_barrier(jnp.sum(d_result, axis=0)), lax.optimization_barrier(jnp.sum(d_pre, axis=0)))
    return (d_mid, d_att, (g_out, g_up, g_down), sums)

def input_backward(d_mid, d_query, d_keys, d_values, early, params, sums):
    w_qkv, w_out, w_up, w_down, gains, biases, up_bias = params
    gain = gains.astype(jnp.float32)
    normed, inv, a_one = early
    d_query_s = d_query * SCALE
    d_proj = jnp.concatenate([d_query_s, d_keys, d_values], axis=1).astype(jnp.bfloat16)
    g_qkv = outer(a_one, d_proj)
    d_a_one = through(d_proj, w_qkv)
    d_input = d_mid + norm_back(d_a_one * gain[0], normed, inv)
    gain_two, shift_two, out_sum, down_sum, up_sum = sums
    g_gains = jnp.stack([lax.optimization_barrier(jnp.sum(d_a_one * normed, axis=0)), gain_two])
    g_biases = jnp.stack([lax.optimization_barrier(jnp.sum(d_a_one, axis=0)), lax.optimization_barrier(jnp.sum(d_query_s, axis=0)), lax.optimization_barrier(jnp.sum(d_values, axis=0)), out_sum, shift_two, down_sum])
    return (d_input, g_qkv, g_gains, g_biases, up_sum)

def split_heads(array):
    return array.reshape(array.shape[0], HEADS, HD).transpose(1, 0, 2)

def merge_heads(array):
    return array.transpose(1, 0, 2).reshape(array.shape[1], HEADS * HD)

def reference(inputs, block_order, w_qkv, w_out, w_up, w_down, norm_gains, biases, up_bias, out_grad):
    offsets = jnp.arange(BLK, dtype=jnp.int32)
    positions = (block_order.astype(jnp.int32)[:, None] * BLK + offsets[None, :]).reshape(-1)
    seq_in = inputs.reshape(SEQS, LENGTH, D)
    seq_grad = out_grad.reshape(SEQS, LENGTH, D)

    def layer_params(index):
        return (w_qkv[index], w_out[index], w_up[index], w_down[index], norm_gains[index], biases[index], up_bias[index])

    def one_sequence(totals, pair):
        x, d_result = pair
        saved = []
        for index in range(LAYERS):
            params = layer_params(index)
            early, query, keys, values = before_attention(x, params)
            att, lse = lax.map(lambda t: head_forward(t[0], t[1], t[2], positions, positions), (split_heads(query), split_heads(keys), split_heads(values)))
            attended = merge_heads(att)
            x, late = after_attention(x, attended, params)
            saved.append((early, query, keys, values, attended, lse, late))
        result = x
        layer_grads = [None] * LAYERS
        for index in reversed(range(LAYERS)):
            params = layer_params(index)
            early, query, keys, values, attended, lse, late = saved[index]
            d_mid, d_att, mats, sums = mlp_backward(d_result, attended, late, params)
            d_q, d_k, d_v = lax.map(lambda t: head_backward(t[0], t[1], t[2], t[3], t[4], t[5], positions, positions), (split_heads(query), split_heads(keys), split_heads(values), split_heads(attended), split_heads(d_att), lse))
            d_result, g_qkv, g_gains, g_biases, g_upb = input_backward(d_mid, merge_heads(d_q), merge_heads(d_k), merge_heads(d_v), early, params, sums)
            layer_grads[index] = (g_qkv, mats[0], mats[1], mats[2], g_gains, g_biases, g_upb)
        stacked = tuple((jnp.stack([layer_grads[i][j] for i in range(LAYERS)]) for j in range(7)))
        totals = tuple((a + b for a, b in zip(totals, stacked)))
        return (totals, (result, d_result))
    zeros = (jnp.zeros((LAYERS, D, 3 * D), jnp.float32), jnp.zeros((LAYERS, D, D), jnp.float32), jnp.zeros((LAYERS, D, FF), jnp.float32), jnp.zeros((LAYERS, FF, D), jnp.float32), jnp.zeros((LAYERS, 2, D), jnp.float32), jnp.zeros((LAYERS, 6, D), jnp.float32), jnp.zeros((LAYERS, FF), jnp.float32))
    totals, (results, d_inputs) = lax.scan(one_sequence, zeros, (seq_in, seq_grad))
    shape = (SEQS, BLOCKS, BLK, D)
    return (results.reshape(shape), d_inputs.reshape(shape), totals[0], totals[1], totals[2], totals[3], totals[4], totals[5], totals[6])
```

```python
import jax
import jax.numpy as jnp
from jax import lax
from jax.sharding import PartitionSpec as P

HEADS = 16
EPS = 1e-05
SCALE = 0.125
GELU_C = 0.7978845608028654
BF = jnp.bfloat16
F32 = jnp.float32


def normalize(x):
    centred = x - jnp.mean(x, axis=1, keepdims=True)
    inv = lax.rsqrt(jnp.mean(centred * centred, axis=1, keepdims=True) + EPS)
    return (centred * inv, inv)


def norm_back(grad, normed, inv):
    return inv * (
        grad
        - jnp.mean(grad, axis=1, keepdims=True)
        - normed * jnp.mean(grad * normed, axis=1, keepdims=True)
    )


def gelu_parts(u):
    inner = GELU_C * (u + 0.044715 * u * u * u)
    tanhed = jnp.tanh(inner)
    value = 0.5 * u * (1.0 + tanhed)
    slope = 0.5 * (1.0 + tanhed) + 0.5 * u * (1.0 - tanhed * tanhed) * GELU_C * (
        1.0 + 3.0 * 0.044715 * u * u
    )
    return (value, slope)


def dot(a, b):
    return jnp.dot(a, b, preferred_element_type=F32)


def outer(left, right):
    return lax.dot_general(left, right, (((0,), (0,)), ((), ())), preferred_element_type=F32)


def through(left, weight):
    return lax.dot_general(left, weight, (((1,), (1,)), ((), ())), preferred_element_type=F32)


def pick(stack, index):
    return lax.dynamic_index_in_dim(stack, index, 0, keepdims=False)


def head_forward(query, keys, values, pos):
    allowed = pos[None, :] <= pos[:, None]
    scores = jnp.where(allowed, through(query, keys), -1e30)
    top = jnp.max(scores, axis=1, keepdims=True)
    lse = top + jnp.log(jnp.sum(jnp.exp(scores - top), axis=1, keepdims=True))
    probs = jnp.exp(scores - lse).astype(BF)
    return (dot(probs, values).astype(BF), lse)


def head_backward(query, keys, values, attended, d_att, lse, pos):
    allowed = pos[None, :] <= pos[:, None]
    scores = through(query, keys)
    probs = jnp.where(allowed, jnp.exp(jnp.where(allowed, scores, 0.0) - lse), 0.0)
    delta = jnp.sum(d_att.astype(F32) * attended.astype(F32), axis=1, keepdims=True)
    d_scores = (probs * (through(d_att, values) - delta)).astype(BF)
    return (dot(d_scores, keys), outer(d_scores, query), outer(probs.astype(BF), d_att))


def build(mesh):
    n_ctx, n_f = mesh.shape["ctx"], mesh.shape["fsdp"]
    n_z = n_ctx // 2

    def fsdp_to(x, k):
        return lax.ppermute(x, "fsdp", [(f, f ^ k) for f in range(n_f)])

    def ctx_to(x, e):
        return lax.ppermute(x, "ctx", [(i, i ^ e) for i in range(n_ctx)])

    def both_to(x, target):
        pairs = []
        for i in range(n_ctx):
            for f in range(n_f):
                to_i, to_f = target(i, f)
                pairs.append((i * n_f + f, to_i * n_f + to_f))
        return lax.ppermute(x, ("ctx", "fsdp"), pairs)

    def on_device(inputs, block_order, w_qkv, w_out, w_up, w_down, gains, biases, up_bias, out_grad):
        seqs, slots, blk, width = inputs.shape
        rows = seqs * slots * blk
        ci = lax.axis_index("ctx")
        fi = lax.axis_index("fsdp")
        z, c = ci // 2, ci % 2
        mine = 2 * fi + c
        wide = width // n_f
        pair = wide // 2
        hidden = up_bias.shape[1]
        head = width // HEADS
        x = inputs.reshape(rows, width)
        d_result = out_grad.reshape(rows, width)
        w_qkv, w_out, w_up, w_down = w_qkv[0], w_out[0], w_up[0], w_down[0]

        def gather_f(block):
            return [block] + [fsdp_to(block, k) for k in range(1, n_f)]

        def natural(parts, axis):
            stack = jnp.stack(parts)
            return jnp.concatenate([pick(stack, b ^ fi) for b in range(n_f)], axis=axis)

        def split_rows(block_of):
            half = w_qkv.shape[0] // 2
            parts = [block_of(fi, None)]
            for k in range(1, n_f):
                got = fsdp_to(block_of(fi ^ k, c), k)
                other = ctx_to(got, 1)
                parts.append(
                    jnp.where(c == 0, jnp.concatenate([got, other]), jnp.concatenate([other, got]))
                )
            return natural(parts, 0)

        def halves(stack):
            def block_of(dest, core):
                block = pick(stack, dest)
                if core is None:
                    return block
                return pick(block.reshape(2, block.shape[0] // 2, block.shape[1]), core)
            return block_of

        small = jnp.concatenate([gains[0], biases[0]])
        small = natural(gather_f(small), 1).astype(F32)
        gain, shift = small[:2], small[2:]

        qkv_cols = w_qkv.reshape(wide, 3, n_f, 2, pair).transpose(2, 0, 3, 1, 4)
        full_qkv = split_rows(halves(qkv_cols.reshape(n_f, wide, 6 * pair)))
        normed, inv = normalize(x)
        a_one = (normed * gain[0] + shift[0]).astype(BF)
        a_all = jnp.concatenate(gather_f(a_one))

        up_cols = w_up.reshape(wide, n_f, hidden).transpose(1, 0, 2)
        full_up = split_rows(halves(up_cols))
        full_out = split_rows(halves(jnp.broadcast_to(w_out, (n_f,) + w_out.shape)))
        dz = d_result.astype(BF)
        dz_all = jnp.concatenate(gather_f(dz))

        proj = dot(a_all, full_qkv).reshape(n_f * rows, 2, 3, pair)
        q_shift = lax.dynamic_slice_in_dim(shift[1], fi * wide, wide).reshape(2, pair)
        v_shift = lax.dynamic_slice_in_dim(shift[2], fi * wide, wide).reshape(2, pair)
        proj = jnp.stack(
            [(proj[:, :, 0] + q_shift) * SCALE, proj[:, :, 1], proj[:, :, 2] + v_shift], axis=2
        ).astype(BF)
        proj = proj.reshape(n_f, rows, 2, 3 * pair).transpose(0, 2, 1, 3)
        proj = proj.reshape(2 * n_f, rows, 3 * pair)
        got = []
        for e in range(n_ctx):
            block = pick(proj, 2 * (fi ^ z ^ (e >> 1)) + (c ^ (e & 1)))
            got.append(ctx_to(block, e) if e else block)
        seq = jnp.concatenate(got)
        length = seq.shape[0]
        query, keys, values = seq[:, :pair], seq[:, pair : 2 * pair], seq[:, 2 * pair :]
        offsets = jnp.arange(blk, dtype=jnp.int32)
        all_pos = (block_order[:, None] * blk + offsets[None, :]).reshape(n_ctx, rows)
        pos = jnp.concatenate([pick(all_pos, ci ^ e) for e in range(n_ctx)])

        outs = []
        for h in range(pair // head):
            cut = slice(h * head, (h + 1) * head)
            outs.append(head_forward(query[:, cut], keys[:, cut], values[:, cut], pos))
        att = jnp.concatenate([o for o, _ in outs], axis=1)

        att_blocks = att.reshape(n_ctx, rows, pair)
        got = []
        for e in range(n_ctx):
            block = pick(att_blocks, ci ^ e ^ mine)
            got.append(both_to(block, lambda i, f: (e ^ (2 * f + i % 2), i // 2)))
        got = jnp.stack(got)
        attended = jnp.concatenate([pick(got, ci ^ b) for b in range(n_ctx)], axis=1)

        mid = x + dot(attended, full_out) + shift[3]
        normed2, inv2 = normalize(mid)
        a_two = (normed2 * gain[1] + shift[4]).astype(BF)
        a2_all = jnp.concatenate(gather_f(a_two))
        pre = dot(a2_all, full_up) + up_bias.astype(F32)
        value, slope = gelu_parts(pre)
        gelled = value.astype(BF)

        def reduce_f(partial):
            parts = partial.reshape(n_f, rows, width)
            total = parts[0]
            for k in range(1, n_f):
                total = total + fsdp_to(parts[k].astype(BF), k).astype(F32)
            return total

        result = mid + reduce_f(dot(gelled, w_down)) + shift[5]

        d_pre = through(dz_all, w_down) * slope
        d_hidden = d_pre.astype(BF)
        d_a_two = reduce_f(through(d_hidden, full_up))
        g_down = outer(gelled, dz_all)
        g_up = outer(a2_all, d_hidden)

        def sum_ctx(blocks):
            by_core = blocks.reshape(n_z, 2, *blocks.shape[1:]).transpose(1, 0, 2, 3)
            half = pick(by_core, c) + ctx_to(pick(by_core, 1 - c).astype(BF), 1).astype(F32)
            total = pick(half, z)
            for m in range(1, n_z):
                total = total + ctx_to(pick(half, z ^ m).astype(BF), 2 * m).astype(F32)
            return total

        def rows_from_columns(blocks):
            blocks = blocks.reshape(n_f, -1, blocks.shape[-1])
            parts = [pick(blocks, fi)]
            for k in range(1, n_f):
                parts.append(fsdp_to(pick(blocks, fi ^ k).astype(BF), k).astype(F32))
            stack = jnp.stack(parts)
            return jnp.stack([pick(stack, b ^ fi) for b in range(n_f)], axis=1)

        d_mid = d_result + norm_back(d_a_two * gain[1], normed2, inv2)
        dy = d_mid.astype(BF)
        d_att = through(dy, full_out).astype(BF)
        d_blocks = d_att.reshape(rows, n_ctx, pair).transpose(1, 0, 2)
        got = []
        for e in range(n_ctx):
            block = pick(d_blocks, ci ^ e)
            got.append(both_to(block, lambda i, f: (2 * f + ((i ^ e) & 1), (i ^ e) >> 1)))
        got = jnp.stack(got)
        d_seq = jnp.concatenate([pick(got, ci ^ b ^ mine) for b in range(n_ctx)])

        grads = []
        for h in range(pair // head):
            cut = slice(h * head, (h + 1) * head)
            grads.append(
                head_backward(
                    query[:, cut], keys[:, cut], values[:, cut],
                    att[:, cut], d_seq[:, cut], outs[h][1], pos,
                )
            )
        d_q = jnp.concatenate([g[0] for g in grads], axis=1) * SCALE
        d_k = jnp.concatenate([g[1] for g in grads], axis=1)
        d_v = jnp.concatenate([g[2] for g in grads], axis=1)
        d_qkv = jnp.concatenate([d_q, d_k, d_v], axis=1).astype(BF).reshape(n_ctx, rows, 3 * pair)
        got = jnp.stack([d_qkv[0]] + [ctx_to(d_qkv[e], e) for e in range(1, n_ctx)])
        d_proj = jnp.concatenate(
            [
                jnp.concatenate([pick(got, 2 * (fi ^ z ^ k) + (c ^ p)) for p in range(2)], axis=1)
                for k in range(n_f)
            ]
        )
        d_a_one = reduce_f(through(d_proj, full_qkv))
        g_qkv = outer(a_all, d_proj)
        d_input = d_mid + norm_back(d_a_one * gain[0], normed, inv)

        out_up = rows_from_columns(sum_ctx(g_up.reshape(n_ctx, -1, hidden)))
        out_up = out_up.reshape(out_up.shape[0], n_f * hidden)
        out_qkv = rows_from_columns(sum_ctx(g_qkv.reshape(n_ctx, -1, 6 * pair)))
        out_qkv = out_qkv.reshape(-1, n_f, 2, 3, pair).transpose(0, 3, 1, 2, 4)
        out_qkv = out_qkv.reshape(-1, 3 * width)
        out_down = both_to(
            sum_ctx(g_down.reshape(n_ctx, -1, width)).astype(BF),
            lambda i, f: ((f * n_ctx + i) // n_f, (f * n_ctx + i) % n_f),
        ).astype(F32)

        def sum_all(blocks):
            by_f = blocks.reshape(n_z, 2, n_f, *blocks.shape[2:])
            own = lax.dynamic_index_in_dim(by_f, c, 1, keepdims=False)
            away = lax.dynamic_index_in_dim(by_f, 1 - c, 1, keepdims=False)
            half = own + ctx_to(away.astype(BF), 1).astype(F32)
            half = half.transpose(1, 0, 2, 3)
            part = pick(half, fi)
            for k in range(1, n_f):
                part = part + fsdp_to(pick(half, fi ^ k).astype(BF), k).astype(F32)
            total = pick(part, z)
            for m in range(1, n_z):
                total = total + ctx_to(pick(part, z ^ m).astype(BF), 2 * m).astype(F32)
            return total

        g_out = outer(attended, dy)
        out_out = sum_all(g_out.reshape(n_ctx, n_f, -1, width))

        def placed(vector):
            spread = jnp.zeros((width,), F32)
            return lax.dynamic_update_slice_in_dim(spread, vector, mine * pair, 0)

        sums = jnp.stack(
            [
                jnp.sum(d_a_one * normed, axis=0),
                jnp.sum(d_a_two * normed2, axis=0),
                jnp.sum(d_a_one, axis=0),
                placed(jnp.sum(d_q, axis=0)),
                placed(jnp.sum(d_v, axis=0)),
                jnp.sum(d_mid, axis=0),
                jnp.sum(d_a_two, axis=0),
                jnp.sum(d_result, axis=0),
            ]
        )
        per = width // (n_ctx * n_f)
        sums = sums.reshape(8, n_ctx, n_f, per).transpose(1, 2, 0, 3).reshape(n_ctx, n_f, 1, 8 * per)
        out_small = sum_all(sums).reshape(8, per)
        up_sum = jnp.sum(d_pre, axis=0).reshape(n_ctx, 1, -1)
        out_upb = both_to(
            sum_ctx(up_sum),
            lambda i, f: ((f * n_ctx + i) // n_f, (f * n_ctx + i) % n_f),
        )
        shape = (seqs, slots, blk, width)
        return (
            result.reshape(shape),
            d_input.reshape(shape),
            out_qkv[None],
            out_out[None],
            out_up[None],
            out_down[None],
            out_small[:2][None],
            out_small[2:][None],
            out_upb.reshape(1, -1),
        )

    return on_device


def solution(mesh):
    return jax.shard_map(
        build(mesh),
        mesh=mesh,
        in_specs=(
            P("fsdp", "ctx", None, None),
            P(),
            P(None, "fsdp", None),
            P(None, "fsdp", None),
            P(None, "fsdp", None),
            P(None, "fsdp", None),
            P(None, None, "fsdp"),
            P(None, None, "fsdp"),
            P(None, "fsdp"),
            P("fsdp", "ctx", None, None),
        ),
        out_specs=(
            P("fsdp", "ctx", None, None),
            P("fsdp", "ctx", None, None),
            P(None, ("ctx", "fsdp"), None),
            P(None, ("ctx", "fsdp"), None),
            P(None, ("ctx", "fsdp"), None),
            P(None, ("ctx", "fsdp"), None),
            P(None, None, ("ctx", "fsdp")),
            P(None, None, ("ctx", "fsdp")),
            P(None, ("ctx", "fsdp")),
        ),
        check_vma=False,
    )
```

```python
import jax
import jax.numpy as jnp
from jax import lax
from jax.experimental import pallas as pl
from jax.experimental.pallas import tpu as pltpu
from jax.sharding import PartitionSpec as P

HEADS = 16
EPS = 1e-05
SCALE = 0.125
GELU_C = 0.7978845608028654
BF = jnp.bfloat16
F32 = jnp.float32


CI, FI, Z, CORE, MINE, ORDER = 0, 1, 2, 3, 4, 8


def normalize(x):
    centred = x - jnp.mean(x, axis=1, keepdims=True)
    inv = lax.rsqrt(jnp.mean(centred * centred, axis=1, keepdims=True) + EPS)
    return (centred * inv, inv)


def norm_back(grad, normed, inv):
    return inv * (
        grad
        - jnp.mean(grad, axis=1, keepdims=True)
        - normed * jnp.mean(grad * normed, axis=1, keepdims=True)
    )


def gelu_parts(u):
    inner = GELU_C * (u + 0.044715 * u * u * u)
    tanhed = jnp.tanh(inner)
    value = 0.5 * u * (1.0 + tanhed)
    slope = 0.5 * (1.0 + tanhed) + 0.5 * u * (1.0 - tanhed * tanhed) * GELU_C * (
        1.0 + 3.0 * 0.044715 * u * u
    )
    return (value, slope)


def dot(a, b):
    return jnp.dot(a, b, preferred_element_type=F32)


def outer(left, right):
    return lax.dot_general(left, right, (((0,), (0,)), ((), ())), preferred_element_type=F32)


def through(left, weight):
    return lax.dot_general(left, weight, (((1,), (1,)), ((), ())), preferred_element_type=F32)


def pick(stack, index):
    return lax.dynamic_index_in_dim(stack, index, 0, keepdims=False)


def shaped(shape, kind):
    return jax.ShapeDtypeStruct(shape, kind)


def total_bytes(arrays):
    return sum(a.size * a.dtype.itemsize for a in arrays)


def call(kernel, name, outs, idx, ins, scratch=(), flops=0):
    vmem = pl.BlockSpec(memory_space=pltpu.VMEM)
    return pl.pallas_call(
        kernel,
        out_shape=outs,
        in_specs=[pl.BlockSpec(memory_space=pltpu.SMEM)] + [vmem] * len(ins),
        out_specs=[vmem] * len(outs),
        scratch_shapes=list(scratch),
        compiler_params=pltpu.CompilerParams(vmem_limit_bytes=48 * 1024 * 1024),
        cost_estimate=pl.CostEstimate(
            flops=flops, bytes_accessed=total_bytes(ins) + total_bytes(outs), transcendentals=0
        ),
        name=name,
    )(idx, *ins)


def build(mesh):
    n_ctx, n_f = mesh.shape["ctx"], mesh.shape["fsdp"]
    n_z = n_ctx // 2

    def fsdp_to(x, k):
        return lax.ppermute(x, "fsdp", [(f, f ^ k) for f in range(n_f)])

    def ctx_to(x, e):
        return lax.ppermute(x, "ctx", [(i, i ^ e) for i in range(n_ctx)])

    def both_to(x, target):
        pairs = []
        for i in range(n_ctx):
            for f in range(n_f):
                to_i, to_f = target(i, f)
                pairs.append((i * n_f + f, to_i * n_f + to_f))
        return lax.ppermute(x, ("ctx", "fsdp"), pairs)

    def gather_f(block):
        return [block] + [fsdp_to(block, k) for k in range(1, n_f)]

    def send_f(blocks):
        return [fsdp_to(b, k + 1) for k, b in enumerate(blocks)]

    def fill_rows(full, own, got, other, fi, core):
        depth = own.shape[0]
        half = depth // 2
        full[pl.ds(fi * depth, depth), :] = own[...]
        for k in range(1, n_f):
            base = (fi ^ k) * depth
            full[pl.ds(base + core * half, half), :] = got[k - 1][:half, :]
            full[pl.ds(base + (1 - core) * half, half), :] = other[k - 1][:half, :]

    def on_device(inputs, block_order, w_qkv, w_out, w_up, w_down, gains, biases, up_bias, out_grad):
        seqs, slots, blk, width = inputs.shape
        rows = seqs * slots * blk
        ci = lax.axis_index("ctx")
        fi = lax.axis_index("fsdp")
        z, c = ci // 2, ci % 2
        mine = 2 * fi + c
        wide = width // n_f
        pair = wide // 2
        hidden = up_bias.shape[1]
        hd = width // HEADS
        heads = pair // hd
        length = n_ctx * rows
        half = wide // 2
        all_rows = n_f * rows
        x = inputs.reshape(rows, width)
        d_result = out_grad.reshape(rows, width)
        w_qkv, w_out, w_up, w_down = w_qkv[0], w_out[0], w_up[0], w_down[0]
        zero = jnp.zeros((), jnp.int32)
        idx = jnp.concatenate(
            [jnp.stack([ci, fi, z, c, mine, zero, zero, zero]).astype(jnp.int32), block_order]
        )
        own_small = jnp.concatenate([gains[0], biases[0]])
        n_small = own_small.shape[0]

        def prep(i, x_ref, w_ref, s_ref, n_ref, own_ref, *send):
            normed, _ = normalize(x_ref[...])
            n_ref[...] = normed.astype(BF)
            f, core = i[FI], i[CORE]
            for q in range(3):
                to = slice(q * wide, (q + 1) * wide)
                at = pl.multiple_of(q * width + f * wide, wide)
                own_ref[:, to] = w_ref[:, pl.ds(at, wide)]
                for k in range(1, n_f):
                    at = pl.multiple_of(q * width + (f ^ k) * wide, wide)
                    row = pl.multiple_of(core * half, half)
                    send[k - 1][:half, to] = w_ref[pl.ds(row, half), pl.ds(at, wide)]
            for k in range(1, n_f):
                send[k - 1][half : half + n_small, :wide] = s_ref[...]

        outs = [shaped((rows, width), BF), shaped((wide, 3 * wide), BF)]
        outs += [shaped((half + 16, 3 * wide), BF)] * (n_f - 1)
        n_one, own_qkv, *sends = call(prep, "prep", outs, idx, [x, w_qkv, own_small])
        got_qkv = send_f(sends)
        other_qkv = [ctx_to(g, 1) for g in got_qkv]
        n_all = gather_f(n_one)

        def project(i, *refs):
            n_refs, refs = refs[:n_f], refs[n_f:]
            own, s_ref, refs = refs[0], refs[1], refs[2:]
            got, refs = refs[: n_f - 1], refs[n_f - 1 :]
            other, refs = refs[: n_f - 1], refs[n_f - 1 :]
            a_ref, full, small, refs = refs[0], refs[1], refs[2], refs[3:]
            send, held = refs[:n_ctx], refs[n_ctx]
            f, core = i[FI], i[CORE]
            for k in range(n_f):
                piece = s_ref[...] if k == 0 else got[k - 1][half : half + n_small, :wide]
                small[:, pl.ds(pl.multiple_of((f ^ k) * wide, wide), wide)] = piece.astype(F32)
            fill_rows(full, own, got, other, f, core)
            at = pl.ds(pl.multiple_of(f * wide, wide), wide)
            q_shift, v_shift = small[3:4, at], small[4:5, at]
            for k in range(n_f):
                a_one = (n_refs[k][...].astype(F32) * small[0:1, :] + small[2:3, :]).astype(BF)
                a_ref[k * rows : (k + 1) * rows, :] = a_one
                proj = dot(a_one, full[...])
                query = ((proj[:, :wide] + q_shift) * SCALE).astype(BF)
                keys = proj[:, wide : 2 * wide].astype(BF)
                values = (proj[:, 2 * wide :] + v_shift).astype(BF)
                for p in range(2):
                    cut = slice(p * pair, (p + 1) * pair)
                    for q, part in enumerate((query, keys, values)):
                        held[k, p, :, q * pair : (q + 1) * pair] = part[:, cut]
            for e in range(n_ctx):
                send[e][...] = held[i[FI] ^ i[Z] ^ (e >> 1), core ^ (e & 1)]

        outs = [
            shaped((all_rows, width), BF),
            shaped((width, 3 * wide), BF),
            shaped((n_small, width), F32),
        ] + [shaped((rows, 3 * pair), BF)] * n_ctx
        a_all, full_qkv, small, *sends = call(
            project, "project", outs, idx,
            n_all + [own_qkv, own_small] + got_qkv + other_qkv,
            [pltpu.VMEM((n_f, 2, rows, 3 * pair), BF)],
            flops=6 * all_rows * width * wide,
        )
        got = [sends[0]] + [ctx_to(sends[e], e) for e in range(1, n_ctx)]

        def cut_weights(i, up_ref, out_ref, own_ref, half_ref, *send):
            f, core = i[FI], i[CORE]
            row = pl.ds(pl.multiple_of(core * half, half), half)
            own_ref[...] = up_ref[:, pl.ds(pl.multiple_of(f * hidden, hidden), hidden)]
            half_ref[...] = out_ref[row, :]
            for k in range(1, n_f):
                at = pl.ds(pl.multiple_of((f ^ k) * hidden, hidden), hidden)
                send[k - 1][...] = up_ref[row, at]

        w_up, w_out, _ = lax.optimization_barrier((w_up, w_out, got[1]))
        outs = [shaped((wide, hidden), BF), shaped((half, width), BF)]
        outs += [shaped((half, hidden), BF)] * (n_f - 1)
        own_up, out_half, *sends = call(cut_weights, "cut", outs, idx, [w_up, w_out])
        got_out = send_f([out_half] * (n_f - 1))
        got_up = send_f(sends)
        got, got_out, got_up = lax.optimization_barrier((got, got_out, got_up))
        other_out = [ctx_to(g, 1) for g in got_out]
        other_up = [ctx_to(g, 1) for g in got_up]

        def positions(i, block, along):
            dims = (rows, 1) if along == 0 else (1, rows)
            at = lax.broadcasted_iota(jnp.int32, dims, along)
            pos = at + i[ORDER + block * slots] * blk
            for s in range(1, slots):
                moved = at - s * blk + i[ORDER + block * slots + s] * blk
                pos = jnp.where(at >= s * blk, moved, pos)
            return pos

        def fill_positions(i, kpos):
            for e in range(n_ctx):
                kpos[:, e * rows : (e + 1) * rows] = positions(i, i[CI] ^ e, 1)

        def attend(i, *refs):
            got, refs = refs[:n_ctx], refs[n_ctx:]
            seq, att, lse_ref, refs = refs[0], refs[1], refs[2], refs[3:]
            send, kpos = refs[:n_ctx], refs[n_ctx]
            for e in range(n_ctx):
                seq[e * rows : (e + 1) * rows, :] = got[e][...]
            fill_positions(i, kpos)

            def step(e, _):
                here = pl.ds(pl.multiple_of(e * rows, rows), rows)
                allowed = kpos[...] <= positions(i, i[CI] ^ e, 0)
                for h in range(heads):
                    cut = slice(h * hd, (h + 1) * hd)
                    keys = seq[:, pair + h * hd : pair + (h + 1) * hd]
                    values = seq[:, 2 * pair + h * hd : 2 * pair + (h + 1) * hd]
                    scores = jnp.where(allowed, through(seq[here, cut], keys), -1e30)
                    top = jnp.max(scores, axis=1, keepdims=True)
                    probs = jnp.exp(scores - top)
                    norm = jnp.sum(probs, axis=1, keepdims=True)
                    out = dot(probs.astype(BF), values) / norm
                    att[here, cut] = out.astype(BF)
                    lse_ref[here, cut] = jnp.broadcast_to(top + jnp.log(norm), (rows, hd))
                return 0

            lax.fori_loop(0, n_ctx, step, 0)
            for e in range(n_ctx):
                at = pl.multiple_of((i[CI] ^ e ^ i[MINE]) * rows, rows)
                send[e][...] = att[pl.ds(at, rows), :]

        outs = [shaped((length, 3 * pair), BF), shaped((length, pair), BF), shaped((length, pair), F32)]
        outs += [shaped((rows, pair), BF)] * n_ctx
        seq, att, lse, *sends = call(
            attend, "attend", outs, idx, got, [pltpu.VMEM((1, length), jnp.int32)],
            flops=4 * length * length * pair,
        )
        got = [
            both_to(sends[e], lambda i, f: (e ^ (2 * f + i % 2), i // 2)) for e in range(n_ctx)
        ]

        def finish(i, *refs):
            x_ref, small_ref, refs = refs[0], refs[1], refs[2:]
            o_refs, refs = refs[:n_ctx], refs[n_ctx:]
            own, refs = refs[0], refs[1:]
            got_o, refs = refs[: n_f - 1], refs[n_f - 1 :]
            other_o, refs = refs[: n_f - 1], refs[n_f - 1 :]
            mid_ref, a_ref, full = refs
            fill_rows(full, own, got_o, other_o, i[FI], i[CORE])
            mid = x_ref[...] + small_ref[5:6, :]
            for e in range(n_ctx):
                at = pl.multiple_of((i[CI] ^ e) * pair, pair)
                mid = mid + dot(o_refs[e][...], full[pl.ds(at, pair), :])
            mid_ref[...] = mid
            normed, _ = normalize(mid)
            a_ref[...] = (normed * small_ref[1:2, :] + small_ref[6:7, :]).astype(BF)

        outs = [shaped((rows, width), F32), shaped((rows, width), BF), shaped((width, width), BF)]
        o_parts = got
        mid, a_two, full_out = call(
            finish, "finish", outs, idx,
            [x, small] + got + [w_out] + got_out + other_out,
            flops=2 * rows * width * width,
        )
        a2_parts = gather_f(a_two)
        dz, _ = lax.optimization_barrier((d_result.astype(BF), a2_parts[1]))
        dz_parts = gather_f(dz)

        def forward(i, *refs):
            a_refs, refs = refs[:n_f], refs[n_f:]
            own, bias, refs = refs[0], refs[1], refs[2:]
            got_u, refs = refs[: n_f - 1], refs[n_f - 1 :]
            other_u, refs = refs[: n_f - 1], refs[n_f - 1 :]
            full, a_ref, gel, slope_ref = refs
            fill_rows(full, own, got_u, other_u, i[FI], i[CORE])
            for k in range(n_f):
                here = slice(k * rows, (k + 1) * rows)
                a_ref[here, :] = a_refs[k][...]
                value, slope = gelu_parts(dot(a_refs[k][...], full[...]) + bias[...].astype(F32))
                gel[here, :] = value.astype(BF)
                slope_ref[here, :] = slope

        outs = [
            shaped((width, hidden), BF),
            shaped((all_rows, width), BF),
            shaped((all_rows, hidden), BF),
            shaped((all_rows, hidden), F32),
        ]
        full_up, a2_all, gelled, slope = call(
            forward, "forward", outs, idx, a2_parts + [own_up, up_bias] + got_up + other_up,
            flops=2 * all_rows * width * hidden,
        )

        def backward(i, *refs):
            dz_refs, refs = refs[:n_f], refs[n_f:]
            slope_ref, down, up, refs = refs[0], refs[1], refs[2], refs[3:]
            dz_ref, du_ref, sum_ref, own, send = refs[0], refs[1], refs[2], refs[3], refs[4:]
            total = jnp.zeros((1, hidden), F32)
            for k in range(n_f):
                here = slice(k * rows, (k + 1) * rows)
                dz_ref[here, :] = dz_refs[k][...]
                d_pre = through(dz_refs[k][...], down[...]) * slope_ref[here, :]
                total = total + jnp.sum(d_pre, axis=0, keepdims=True)
                d_hidden = d_pre.astype(BF)
                du_ref[here, :] = d_hidden
                part = through(d_hidden, up[...])
                if k:
                    send[k - 1][...] = part.astype(BF)
                else:
                    own[...] = part
            sum_ref[...] = total

        outs = [
            shaped((all_rows, width), BF),
            shaped((all_rows, hidden), BF),
            shaped((1, hidden), F32),
            shaped((rows, width), F32),
        ] + [shaped((rows, width), BF)] * (n_f - 1)
        dz_all, d_hidden, up_sum, d_own, *sends = call(
            backward, "backward", outs, idx, dz_parts + [slope, w_down, full_up],
            flops=4 * all_rows * width * hidden,
        )
        got_a = send_f(sends)
        g_down = outer(gelled, dz_all).astype(BF)
        g_up = outer(a2_all, d_hidden).astype(BF)

        def scatter_ctx(g):
            return lax.psum_scatter(g, "ctx", scatter_dimension=0, tiled=True)

        part_down = scatter_ctx(g_down)
        part_up = scatter_ctx(g_up)

        def second(i, *refs):
            d_ref, mid_ref, small_ref, full, own, refs = (*refs[:5], refs[5:])
            got, refs = refs[: n_f - 1], refs[n_f - 1 :]
            dmid_ref, dy_ref, sums, send = refs[0], refs[1], refs[2], refs[3:]
            d_a = own[...]
            for g in got:
                d_a = d_a + g[...].astype(F32)
            normed, inv = normalize(mid_ref[...])
            d_res = d_ref[...]
            d_mid = d_res + norm_back(d_a * small_ref[1:2, :], normed, inv)
            dmid_ref[...] = d_mid
            dy = d_mid.astype(BF)
            dy_ref[...] = dy
            for e in range(n_ctx):
                at = pl.multiple_of((i[CI] ^ e) * pair, pair)
                send[e][...] = through(dy, full[pl.ds(at, pair), :]).astype(BF)
            sums[...] = jnp.zeros_like(sums)
            sums[1:2, :] = jnp.sum(d_a * normed, axis=0, keepdims=True)
            sums[5:6, :] = jnp.sum(d_mid, axis=0, keepdims=True)
            sums[6:7, :] = jnp.sum(d_a, axis=0, keepdims=True)
            sums[7:8, :] = jnp.sum(d_res, axis=0, keepdims=True)

        outs = [shaped((rows, width), F32), shaped((rows, width), BF), shaped((8, width), F32)]
        outs += [shaped((rows, pair), BF)] * n_ctx
        d_mid, dy, sums, *sends = call(
            second, "second", outs, idx, [d_result, mid, small, full_out, d_own] + got_a,
            flops=2 * rows * width * width,
        )
        got = [
            both_to(sends[e], lambda i, f: (2 * f + ((i ^ e) & 1), (i ^ e) >> 1))
            for e in range(n_ctx)
        ]

        def down(i, gel, w_ref, own, *send):
            for k in range(n_f):
                part = dot(gel[k * rows : (k + 1) * rows, :], w_ref[...])
                if k:
                    send[k - 1][...] = part.astype(BF)
                else:
                    own[...] = part

        gel_late, _ = lax.optimization_barrier((gelled, got[-1]))
        outs = [shaped((rows, width), F32)] + [shaped((rows, width), BF)] * (n_f - 1)
        result, *sends = call(
            down, "down", outs, idx, [gel_late, w_down], flops=2 * all_rows * width * hidden
        )
        result = result + mid + small[7]
        for g in send_f(sends):
            result = result + g.astype(F32)

        def attend_back(i, *refs):
            seq_ref, att_ref, lse_ref, refs = refs[0], refs[1], refs[2], refs[3:]
            got, refs = refs[:n_ctx], refs[n_ctx:]
            sum_ref, refs = refs[0], refs[1:]
            send, (kpos, d_out, d_query, d_keys, d_values) = refs[:n_ctx], refs[n_ctx:]
            fill_positions(i, kpos)
            for e in range(n_ctx):
                at = pl.multiple_of((i[CI] ^ e ^ i[MINE]) * rows, rows)
                d_out[pl.ds(at, rows), :] = got[e][...]
            d_keys[...] = jnp.zeros_like(d_keys)
            d_values[...] = jnp.zeros_like(d_values)

            def step(e, _):
                here = pl.ds(pl.multiple_of(e * rows, rows), rows)
                allowed = kpos[...] <= positions(i, i[CI] ^ e, 0)
                for h in range(heads):
                    cut = slice(h * hd, (h + 1) * hd)
                    query, d_att = seq_ref[here, cut], d_out[here, cut]
                    keys = seq_ref[:, pair + h * hd : pair + (h + 1) * hd]
                    values = seq_ref[:, 2 * pair + h * hd : 2 * pair + (h + 1) * hd]
                    lse = lse_ref[here, h * hd : h * hd + 1]
                    scores = jnp.where(allowed, through(query, keys), -1e30)
                    probs = jnp.exp(scores - lse)
                    delta = jnp.sum(
                        d_att.astype(F32) * att_ref[here, cut].astype(F32), axis=1, keepdims=True
                    )
                    d_scores = (probs * (through(d_att, values) - delta)).astype(BF)
                    d_query[here, cut] = dot(d_scores, keys) * SCALE
                    d_keys[:, cut] += outer(d_scores, query)
                    d_values[:, cut] += outer(probs.astype(BF), d_att)
                return 0

            lax.fori_loop(0, n_ctx, step, 0)
            for e in range(n_ctx):
                here = slice(e * rows, (e + 1) * rows)
                send[e][:, :pair] = d_query[here, :].astype(BF)
                send[e][:, pair : 2 * pair] = d_keys[here, :].astype(BF)
                send[e][:, 2 * pair :] = d_values[here, :].astype(BF)
            sum_ref[...] = jnp.zeros_like(sum_ref)
            sum_ref[3:4, :] = jnp.sum(d_query[...], axis=0, keepdims=True)
            sum_ref[4:5, :] = jnp.sum(d_values[...], axis=0, keepdims=True)

        outs = [shaped((8, pair), F32)] + [shaped((rows, 3 * pair), BF)] * n_ctx
        qv_sum, *sends = call(
            attend_back, "attend_back", outs, idx, [seq, att, lse] + got,
            [
                pltpu.VMEM((1, length), jnp.int32),
                pltpu.VMEM((length, pair), BF),
                pltpu.VMEM((length, pair), F32),
                pltpu.VMEM((length, pair), F32),
                pltpu.VMEM((length, pair), F32),
            ],
            flops=10 * length * length * pair,
        )
        got = [sends[0]] + [ctx_to(sends[e], e) for e in range(1, n_ctx)]

        n_all_dev = n_ctx * n_f
        per = width // n_all_dev

        def grad_out(i, dy_ref, *refs):
            o_refs, (away, keep, held) = refs[:n_ctx], refs[n_ctx:]
            for e in range(n_ctx):
                at = pl.multiple_of((i[CI] ^ e) * pair, pair)
                held[pl.ds(at, pair), :] = outer(o_refs[e][...], dy_ref[...])
            for b in range(n_z):
                for f in range(n_f):
                    at = (2 * b + i[CORE]) * n_f * per + f * per
                    keep[f, b * per : (b + 1) * per, :] = held[pl.ds(at, per), :]
                    at = (2 * b + 1 - i[CORE]) * n_f * per + f * per
                    away[f, b * per : (b + 1) * per, :] = held[pl.ds(at, per), :].astype(BF)

        dims = (n_f, n_z * per, width)
        away, out_keep = call(
            grad_out, "grad_out", [shaped(dims, BF), shaped(dims, F32)], idx, [dy] + o_parts,
            [pltpu.VMEM((width, width), F32)], flops=2 * rows * width * width,
        )
        away = ctx_to(away, 1)

        def out_first(i, keep, got, own, *send):
            f = i[FI]
            own[...] = keep[f] + got[f].astype(F32)
            for k in range(1, n_f):
                send[k - 1][...] = (keep[f ^ k] + got[f ^ k].astype(F32)).astype(BF)

        outs = [shaped((n_z * per, width), F32)] + [shaped((n_z * per, width), BF)] * (n_f - 1)
        out_own, *sends = call(out_first, "out_first", outs, idx, [out_keep, away])
        for g in send_f(sends):
            out_own = out_own + g.astype(F32)
        out_own = out_own.reshape(n_z, per, width)

        def first(i, *refs):
            got, refs = refs[:n_ctx], refs[n_ctx:]
            n_refs, refs = refs[:n_f], refs[n_f:]
            full, sum_in, refs = refs[0], refs[1], refs[2:]
            proj_ref, sums, own, send, held = refs[0], refs[1], refs[2], refs[3:-1], refs[-1]
            for e in range(n_ctx):
                held[e] = got[e][...]
            gain_sum = jnp.zeros((1, width), F32)
            shift_sum = jnp.zeros((1, width), F32)
            for k in range(n_f):
                here = slice(k * rows, (k + 1) * rows)
                for p in range(2):
                    e = 2 * (i[FI] ^ i[Z] ^ k) + (i[CORE] ^ p)
                    for q in range(3):
                        at = q * wide + p * pair
                        proj_ref[here, at : at + pair] = held[e, :, q * pair : (q + 1) * pair]
                part = through(proj_ref[here, :], full[...])
                gain_sum += jnp.sum(part * n_refs[k][...].astype(F32), axis=0, keepdims=True)
                shift_sum += jnp.sum(part, axis=0, keepdims=True)
                if k:
                    send[k - 1][...] = part.astype(BF)
                else:
                    own[...] = part
            sums[...] = sum_in[...]
            sums[0:1, :] = gain_sum
            sums[2:3, :] = shift_sum

        outs = [
            shaped((all_rows, 3 * wide), BF),
            shaped((8, width), F32),
            shaped((rows, width), F32),
        ] + [shaped((rows, width), BF)] * (n_f - 1)
        d_proj, sums, d_own, *sends = call(
            first, "first", outs, idx, got + n_all + [full_qkv, sums],
            [pltpu.VMEM((n_ctx, rows, 3 * pair), BF)],
            flops=6 * all_rows * width * wide,
        )
        got_x = send_f(sends)

        block = width // n_ctx
        per_up = hidden // n_ctx

        def pack(i, a_ref, p_ref, sums_ref, up_ref, qv_ref, away, keep, held):
            f, core = i[FI], i[CORE]
            for zz in range(n_z):
                at = slice(2 * zz * block, 2 * (zz + 1) * block)
                held[...] = outer(a_ref[:, at], p_ref[...])
                both = sums_ref[:, at]
                for par, out in ((core, keep), (1 - core, away)):
                    row = pl.ds(pl.multiple_of(par * block, block), block)
                    out[zz, :block, :] = held[row, :].astype(out.dtype)
                    out[zz, block:, :] = jnp.zeros((16, 3 * wide), out.dtype)
                    hit = jnp.logical_and(zz == f, par == core)
                    small = jnp.where(par == 0, both[:, :block], both[:, block:])
                    small = small + jnp.where(hit, qv_ref[...], 0.0)
                    ups = up_ref[:, pl.ds(pl.multiple_of(par * n_f * per_up, n_f * per_up), n_f * per_up)]
                    ups = jnp.where(zz == f, ups, 0.0)
                    out[zz, block : block + 8, :block] = small.astype(out.dtype)
                    for g in range(n_f):
                        out[zz, block + 8 + g : block + 9 + g, :per_up] = ups[
                            :, g * per_up : (g + 1) * per_up
                        ].astype(out.dtype)

        dims = (n_z, block + 16, 3 * wide)
        away, keep = call(
            pack, "pack", [shaped(dims, BF), shaped(dims, F32)], idx,
            [a_all, d_proj, sums, up_sum, qv_sum], [pltpu.VMEM((2 * block, 3 * wide), F32)],
            flops=6 * all_rows * width * wide,
        )
        away = ctx_to(away, 1)

        def over_core(i, keep_ref, got, own, *send):
            own[...] = keep_ref[i[Z]] + got[i[Z]].astype(F32)
            for m in range(1, n_z):
                at = i[Z] ^ m
                send[m - 1][...] = (keep_ref[at] + got[at].astype(F32)).astype(BF)

        outs = [shaped(dims[1:], F32)] + [shaped(dims[1:], BF)] * (n_z - 1)
        own, *sends = call(over_core, "over_core", outs, idx, [keep, away])
        got = [ctx_to(s, 2 * (m + 1)) for m, s in enumerate(sends)]
        got_o = [
            ctx_to(pick(out_own, z ^ m).astype(BF), 2 * m).astype(F32) for m in range(1, n_z)
        ]
        out_out = pick(out_own, z) + sum(got_o)

        def over_z(i, *refs):
            own_ref, got, refs = refs[0], refs[1:n_z], refs[n_z:]
            own, send, held = refs[0], refs[1:-1], refs[-1]
            total = own_ref[...]
            for g in got:
                total = total + g[...].astype(F32)
            held[...] = total
            for k in range(n_f):
                at = pl.ds(pl.multiple_of((i[FI] ^ k) * per, per), per)
                out = send[k - 1] if k else own
                out[:per, :] = held[at, :].astype(out.dtype)
                out[per:, :] = held[block:, :].astype(out.dtype)

        dims = (per + 16, 3 * wide)
        outs = [shaped(dims, F32)] + [shaped(dims, BF)] * (n_f - 1)
        own, *sends = call(
            over_z, "over_z", outs, idx, [own] + got, [pltpu.VMEM((block + 16, 3 * wide), F32)]
        )
        got = send_f(sends)

        def last(i, own_ref, *refs):
            got, (out, small_ref) = refs[: n_f - 1], refs[n_f - 1 :]
            total = own_ref[per:, :block]
            for k in range(n_f):
                src = got[k - 1] if k else own_ref
                for q in range(3):
                    at = pl.ds(pl.multiple_of(q * width + (i[FI] ^ k) * wide, wide), wide)
                    out[:, at] = src[:per, q * wide : (q + 1) * wide].astype(F32)
                if k:
                    total = total + src[per:, :block].astype(F32)
            small_ref[...] = total

        out_qkv, tile = call(
            last, "last", [shaped((per, 3 * width), F32), shaped((16, block), F32)], idx, [own] + got
        )
        out_small = lax.dynamic_slice(tile, (0, fi * per), (8, per))
        out_upb = lax.dynamic_slice(tile, (8 + fi, 0), (1, per_up))

        def rows_from_columns(blocks):
            blocks = blocks.reshape(n_f, -1, blocks.shape[-1])
            parts = [pick(blocks, fi)]
            for k in range(1, n_f):
                parts.append(fsdp_to(pick(blocks, fi ^ k), k))
            stack = jnp.stack(parts)
            return jnp.concatenate([pick(stack, b ^ fi) for b in range(n_f)], axis=1)

        out_up = rows_from_columns(part_up).astype(F32)
        out_down = both_to(
            part_down, lambda i, f: ((f * n_ctx + i) // n_f, (f * n_ctx + i) % n_f)
        ).astype(F32)

        normed, inv = normalize(x)
        d_a = d_own
        for g in got_x:
            d_a = d_a + g.astype(F32)
        d_input = d_mid + norm_back(d_a * small[0], normed, inv)

        shape = (seqs, slots, blk, width)
        return (
            result.reshape(shape),
            d_input.reshape(shape),
            out_qkv[None],
            out_out[None],
            out_up[None],
            out_down[None],
            out_small[:2][None],
            out_small[2:][None],
            out_upb.reshape(1, -1),
        )

    return on_device


def solution(mesh):
    return jax.shard_map(
        build(mesh),
        mesh=mesh,
        in_specs=(
            P("fsdp", "ctx", None, None),
            P(),
            P(None, "fsdp", None),
            P(None, "fsdp", None),
            P(None, "fsdp", None),
            P(None, "fsdp", None),
            P(None, None, "fsdp"),
            P(None, None, "fsdp"),
            P(None, "fsdp"),
            P("fsdp", "ctx", None, None),
        ),
        out_specs=(
            P("fsdp", "ctx", None, None),
            P("fsdp", "ctx", None, None),
            P(None, ("ctx", "fsdp"), None),
            P(None, ("ctx", "fsdp"), None),
            P(None, ("ctx", "fsdp"), None),
            P(None, ("ctx", "fsdp"), None),
            P(None, None, ("ctx", "fsdp")),
            P(None, None, ("ctx", "fsdp")),
            P(None, ("ctx", "fsdp")),
        ),
        check_vma=False,
    )
```

```python
import jax
import jax.numpy as jnp
from jax import lax
from jax.experimental import pallas as pl
from jax.experimental.pallas import tpu as pltpu
from jax.sharding import PartitionSpec as P


HEADS = 16
EPS = 1e-05
SCALE = 0.125
GELU_C = 0.7978845608028654
BF = jnp.bfloat16
F32 = jnp.float32


CI, FI, Z, CORE, ORDER = 0, 1, 2, 3, 8


def normalize(x):
    centred = x - jnp.mean(x, axis=1, keepdims=True)
    inv = lax.rsqrt(jnp.mean(centred * centred, axis=1, keepdims=True) + EPS)
    return (centred * inv, inv)


def norm_back(grad, normed, inv):
    return inv * (
        grad
        - jnp.mean(grad, axis=1, keepdims=True)
        - normed * jnp.mean(grad * normed, axis=1, keepdims=True)
    )


def gelu_parts(u):
    inner = GELU_C * (u + 0.044715 * u * u * u)
    tanhed = jnp.tanh(inner)
    value = 0.5 * u * (1.0 + tanhed)
    slope = 0.5 * (1.0 + tanhed) + 0.5 * u * (1.0 - tanhed * tanhed) * GELU_C * (
        1.0 + 3.0 * 0.044715 * u * u
    )
    return (value, slope)


def dot(a, b):
    return jnp.dot(a, b, preferred_element_type=F32)


def outer(left, right):
    return lax.dot_general(left, right, (((0,), (0,)), ((), ())), preferred_element_type=F32)


def through(left, weight):
    return lax.dot_general(left, weight, (((1,), (1,)), ((), ())), preferred_element_type=F32)


def shaped(shape, kind):
    return jax.ShapeDtypeStruct(shape, kind)


def total_bytes(arrays):
    return sum(a.size * a.dtype.itemsize for a in arrays)


def call(kernel, outs, idx, ins, scratch=(), flops=0):
    vmem = pl.BlockSpec(memory_space=pltpu.VMEM)
    return pl.pallas_call(
        kernel,
        out_shape=outs,
        in_specs=[pl.BlockSpec(memory_space=pltpu.SMEM)] + [vmem] * len(ins),
        out_specs=[vmem] * len(outs),
        scratch_shapes=list(scratch),
        compiler_params=pltpu.CompilerParams(vmem_limit_bytes=20 * 1024 * 1024),
        cost_estimate=pl.CostEstimate(
            flops=flops, bytes_accessed=total_bytes(ins) + total_bytes(outs), transcendentals=0
        ),
    )(idx, *ins)


def build(mesh):
    n_ctx, n_f = mesh.shape["ctx"], mesh.shape["fsdp"]
    n_z = n_ctx // 2

    def fsdp_to(x, k):
        return lax.ppermute(x, "fsdp", [(f, f ^ k) for f in range(n_f)])

    def ctx_to(x, e):
        return lax.ppermute(x, "ctx", [(i, i ^ e) for i in range(n_ctx)])

    def both_to(x, target):
        pairs = []
        for i in range(n_ctx):
            for f in range(n_f):
                to_i, to_f = target(i, f)
                pairs.append((i * n_f + f, to_i * n_f + to_f))
        return lax.ppermute(x, ("ctx", "fsdp"), pairs)

    def gather_f(block):
        return [block] + [fsdp_to(block, k) for k in range(1, n_f)]

    def send_f(blocks):
        return [fsdp_to(b, k + 1) for k, b in enumerate(blocks)]

    def share_core(blocks):
        return [ctx_to(b, 1) for b in blocks]

    def fill_rows(full, own, got, other, fi, core, cut=slice(None)):
        depth = own.shape[0]
        half = depth // 2
        full[pl.ds(fi * depth, depth), :] = own[:, cut]
        for k in range(1, n_f):
            base = (fi ^ k) * depth
            full[pl.ds(base + core * half, half), :] = got[k - 1][:half, cut]
            full[pl.ds(base + (1 - core) * half, half), :] = other[k - 1][:half, cut]

    def layer(inputs, block_order, w_qkv, w_out, w_up, w_down, gains, biases, up_bias, out_grad):
        seqs, slots, blk, width = inputs.shape
        rows = seqs * slots * blk
        ci = lax.axis_index("ctx")
        fi = lax.axis_index("fsdp")
        z, c = ci // 2, ci % 2
        mine = 2 * fi + c
        wide = width // n_f
        pair = wide // 2
        hidden = up_bias.shape[1]
        hd = width // HEADS
        heads = pair // hd
        length = n_ctx * rows
        half = wide // 2
        all_rows = n_f * rows
        x = inputs.reshape(rows, width)
        d_result = out_grad.reshape(rows, width)
        w_qkv, w_out, w_up, w_down = w_qkv[0], w_out[0], w_up[0], w_down[0]
        zero = jnp.zeros((), jnp.int32)
        idx = jnp.concatenate(
            [jnp.stack([ci, fi, z, c, mine, zero, zero, zero]).astype(jnp.int32), block_order]
        )
        own_small = jnp.concatenate([gains[0], biases[0]])
        n_small = own_small.shape[0]

        def prep(i, x_ref, w_ref, s_ref, n_ref, own_ref, *send):
            normed, _ = normalize(x_ref[...])
            n_ref[...] = normed.astype(BF)
            f, core = i[FI], i[CORE]
            for q in range(3):
                to = slice(q * wide, (q + 1) * wide)
                at = pl.multiple_of(q * width + f * wide, wide)
                own_ref[:, to] = w_ref[:, pl.ds(at, wide)]
                for k in range(1, n_f):
                    at = pl.multiple_of(q * width + (f ^ k) * wide, wide)
                    row = pl.multiple_of(core * half, half)
                    send[k - 1][:half, to] = w_ref[pl.ds(row, half), pl.ds(at, wide)]
            for k in range(1, n_f):
                send[k - 1][half : half + n_small, :wide] = s_ref[...]

        outs = [shaped((rows, width), BF), shaped((wide, 3 * wide), BF)]
        outs += [shaped((half + 16, 3 * wide), BF)] * (n_f - 1)
        n_one, own_qkv, *sends = call(prep, outs, idx, [x, w_qkv, own_small])
        got_qkv = send_f(sends)
        other_qkv = share_core(got_qkv)
        n_all = gather_f(n_one)

        def project(i, *refs):
            n_refs, refs = refs[:n_f], refs[n_f:]
            own, s_ref, refs = refs[0], refs[1], refs[2:]
            got, refs = refs[: n_f - 1], refs[n_f - 1 :]
            other, refs = refs[: n_f - 1], refs[n_f - 1 :]
            a_ref, full, small, refs = refs[0], refs[1], refs[2], refs[3:]
            send, held = refs[:n_ctx], refs[n_ctx]
            f, core = i[FI], i[CORE]
            for k in range(n_f):
                piece = s_ref[...] if k == 0 else got[k - 1][half : half + n_small, :wide]
                small[:, pl.ds(pl.multiple_of((f ^ k) * wide, wide), wide)] = piece.astype(F32)
            fill_rows(full, own, got, other, f, core)
            at = pl.ds(pl.multiple_of(f * wide, wide), wide)
            q_shift, v_shift = small[3:4, at], small[4:5, at]
            for k in range(n_f):
                a_one = (n_refs[k][...].astype(F32) * small[0:1, :] + small[2:3, :]).astype(BF)
                a_ref[k * rows : (k + 1) * rows, :] = a_one
                proj = dot(a_one, full[...])
                query = ((proj[:, :wide] + q_shift) * SCALE).astype(BF)
                keys = proj[:, wide : 2 * wide].astype(BF)
                values = (proj[:, 2 * wide :] + v_shift).astype(BF)
                for p in range(2):
                    cut = slice(p * pair, (p + 1) * pair)
                    for q, part in enumerate((query, keys, values)):
                        held[k, p, :, q * pair : (q + 1) * pair] = part[:, cut]
            for e in range(n_ctx):
                send[e][...] = held[i[FI] ^ i[Z] ^ (e >> 1), core ^ (e & 1)]

        outs = [
            shaped((all_rows, width), BF),
            shaped((width, 3 * wide), BF),
            shaped((n_small, width), F32),
        ] + [shaped((rows, 3 * pair), BF)] * n_ctx
        a_all, full_qkv, small, *sends = call(
            project, outs, idx,
            n_all + [own_qkv, own_small] + got_qkv + other_qkv,
            [pltpu.VMEM((n_f, 2, rows, 3 * pair), BF)],
            flops=6 * all_rows * width * wide,
        )
        got = [sends[0]] + [ctx_to(sends[e], e) for e in range(1, n_ctx)]

        def cut_weights(i, up_ref, out_ref, own_ref, *send):
            f, core = i[FI], i[CORE]
            row = pl.ds(pl.multiple_of(core * half, half), half)
            own_ref[:, :hidden] = up_ref[:, pl.ds(pl.multiple_of(f * hidden, hidden), hidden)]
            own_ref[:, hidden:] = out_ref[...]
            for k in range(1, n_f):
                at = pl.ds(pl.multiple_of((f ^ k) * hidden, hidden), hidden)
                send[k - 1][:, :hidden] = up_ref[row, at]
                send[k - 1][:, hidden:] = out_ref[row, :]

        outs = [shaped((wide, hidden + width), BF)]
        outs += [shaped((half, hidden + width), BF)] * (n_f - 1)
        own_w, *sends = call(cut_weights, outs, idx, [w_up, w_out])
        got_w = send_f(sends)
        other_w = share_core(got_w)
        dz, _ = lax.optimization_barrier((d_result.astype(BF), n_all))
        dz_all = lax.all_gather(dz, "fsdp", axis=0, tiled=True)

        def positions(i, block, along):
            dims = (rows, 1) if along == 0 else (1, rows)
            at = lax.broadcasted_iota(jnp.int32, dims, along)
            pos = at + i[ORDER + block * slots] * blk
            for s in range(1, slots):
                moved = at - s * blk + i[ORDER + block * slots + s] * blk
                pos = jnp.where(at >= s * blk, moved, pos)
            return pos

        def fill_positions(i, kpos, qpos):
            for e in range(n_ctx):
                here = slice(e * rows, (e + 1) * rows)
                kpos[:, here] = positions(i, i[CI] ^ e, 1)
                qpos[here, :] = positions(i, i[CI] ^ e, 0)

        tall = 2 * rows
        places = [pltpu.VMEM((1, length), jnp.int32), pltpu.VMEM((length, 1), jnp.int32)]

        def attend(i, *refs):
            got, refs = refs[:n_ctx], refs[n_ctx:]
            seq, att, lse_ref, refs = refs[0], refs[1], refs[2], refs[3:]
            send, (kpos, qpos) = refs[:n_f], refs[n_f:]
            for e in range(n_ctx):
                seq[e * rows : (e + 1) * rows, :] = got[e][...]
            fill_positions(i, kpos, qpos)

            def step(e, _):
                here = pl.ds(pl.multiple_of(e * tall, tall), tall)
                allowed = kpos[...] <= qpos[here, :]
                for h in range(heads):
                    cut = slice(h * hd, (h + 1) * hd)
                    keys = seq[:, pair + h * hd : pair + (h + 1) * hd]
                    values = seq[:, 2 * pair + h * hd : 2 * pair + (h + 1) * hd]
                    scores = jnp.where(allowed, through(seq[here, cut], keys), -1e30)
                    top = jnp.max(scores, axis=1, keepdims=True)
                    probs = jnp.exp(scores - top)
                    norm = jnp.sum(probs, axis=1, keepdims=True)
                    out = dot(probs.astype(BF), values) / norm
                    att[here, cut] = out.astype(BF)
                    lse_ref[here, cut] = jnp.broadcast_to(top + jnp.log(norm), (tall, hd))
                return 0

            lax.fori_loop(0, length // tall, step, 0)
            for m in range(n_f):
                for core in range(2):
                    block = (2 * (m ^ i[FI]) + core) ^ i[CI]
                    at = pl.multiple_of(block * rows, rows)
                    send[m][core * rows : (core + 1) * rows, :] = att[pl.ds(at, rows), :]

        outs = [shaped((length, 3 * pair), BF), shaped((length, pair), BF), shaped((length, pair), F32)]
        outs += [shaped((tall, pair), BF)] * n_f
        seq, att, lse, *sends = call(
            attend, outs, idx, got, places, flops=4 * length * length * pair
        )
        got = [both_to(sends[m], lambda i, f: (2 * (m ^ f) + i % 2, i // 2)) for m in range(n_f)]
        o_parts = got + [ctx_to(g, 1) for g in got]

        def o_part(i, refs, core, m):
            here = pl.ds(pl.multiple_of(i[CORE] * rows, rows), rows)
            own, other = refs[m][here, :], refs[n_f + m][here, :]
            return jnp.where(core == i[CORE], own, other)

        def finish(i, *refs):
            x_ref, small_ref, refs = refs[0], refs[1], refs[2:]
            o_refs, refs = refs[: 2 * n_f], refs[2 * n_f :]
            own, refs = refs[0], refs[1:]
            got_o, refs = refs[: n_f - 1], refs[n_f - 1 :]
            other_o, refs = refs[: n_f - 1], refs[n_f - 1 :]
            mid_ref, a_ref, full = refs
            fill_rows(full, own, got_o, other_o, i[FI], i[CORE], slice(hidden, None))
            mid = x_ref[...] + small_ref[5:6, :]
            for m in range(n_f):
                for core in range(2):
                    at = pl.multiple_of((2 * (m ^ i[Z]) + core) * pair, pair)
                    mid = mid + dot(o_part(i, o_refs, core, m), full[pl.ds(at, pair), :])
            mid_ref[...] = mid
            normed, _ = normalize(mid)
            a_ref[...] = (normed * small_ref[1:2, :] + small_ref[6:7, :]).astype(BF)

        outs = [shaped((rows, width), F32), shaped((rows, width), BF), shaped((width, width), BF)]
        mid, a_two, full_out = call(
            finish, outs, idx,
            [x, small] + o_parts + [own_w] + got_w + other_w,
            flops=2 * rows * width * width,
        )
        a2_parts = gather_f(a_two)

        def forward(i, *refs):
            a_refs, refs = refs[:n_f], refs[n_f:]
            own, bias, refs = refs[0], refs[1], refs[2:]
            got_u, refs = refs[: n_f - 1], refs[n_f - 1 :]
            other_u, refs = refs[: n_f - 1], refs[n_f - 1 :]
            full, a_ref, gel, slope_ref = refs
            fill_rows(full, own, got_u, other_u, i[FI], i[CORE], slice(0, hidden))
            for k in range(n_f):
                here = slice(k * rows, (k + 1) * rows)
                a_ref[here, :] = a_refs[k][...]
                value, slope = gelu_parts(dot(a_refs[k][...], full[...]) + bias[...].astype(F32))
                gel[here, :] = value.astype(BF)
                slope_ref[here, :] = slope

        outs = [
            shaped((width, hidden), BF),
            shaped((all_rows, width), BF),
            shaped((all_rows, hidden), BF),
            shaped((all_rows, hidden), F32),
        ]
        full_up, a2_all, gelled, slope = call(
            forward, outs, idx, a2_parts + [own_w, up_bias] + got_w + other_w,
            flops=2 * all_rows * width * hidden,
        )

        def backward(i, *refs):
            dz_nat, slope_ref, down, up, refs = refs[0], refs[1], refs[2], refs[3], refs[4:]
            dz_ref, du_ref, sum_ref, own, send = refs[0], refs[1], refs[2], refs[3], refs[4:]
            total = jnp.zeros((1, hidden), F32)
            for k in range(n_f):
                here = slice(k * rows, (k + 1) * rows)
                dz_k = dz_nat[pl.ds(pl.multiple_of((i[FI] ^ k) * rows, rows), rows), :]
                dz_ref[here, :] = dz_k
                d_pre = through(dz_k, down[...]) * slope_ref[here, :]
                total = total + jnp.sum(d_pre, axis=0, keepdims=True)
                d_hidden = d_pre.astype(BF)
                du_ref[here, :] = d_hidden
                part = through(d_hidden, up[...])
                if k:
                    send[k - 1][...] = part.astype(BF)
                else:
                    own[...] = part
            sum_ref[...] = total

        outs = [
            shaped((all_rows, width), BF),
            shaped((all_rows, hidden), BF),
            shaped((1, hidden), F32),
            shaped((rows, width), F32),
        ] + [shaped((rows, width), BF)] * (n_f - 1)
        dz_all, d_hidden, up_sum, d_own, *sends = call(
            backward, outs, idx, [dz_all, slope, w_down, full_up],
            flops=4 * all_rows * width * hidden,
        )
        got_a = send_f(sends)
        g_down = outer(gelled, dz_all).astype(BF)
        g_up = outer(a2_all, d_hidden).astype(BF)

        def scatter_ctx(g):
            return lax.psum_scatter(g, "ctx", scatter_dimension=0, tiled=True)

        part_down = scatter_ctx(g_down)
        part_up = scatter_ctx(g_up)

        def second(i, *refs):
            d_ref, mid_ref, small_ref, full, own, refs = (*refs[:5], refs[5:])
            got, refs = refs[: n_f - 1], refs[n_f - 1 :]
            dmid_ref, dy_ref, sums, send = refs[0], refs[1], refs[2], refs[3:]
            d_a = own[...]
            for g in got:
                d_a = d_a + g[...].astype(F32)
            normed, inv = normalize(mid_ref[...])
            d_res = d_ref[...]
            d_mid = d_res + norm_back(d_a * small_ref[1:2, :], normed, inv)
            dmid_ref[...] = d_mid
            dy = d_mid.astype(BF)
            dy_ref[...] = dy
            for m in range(n_f):
                at = pl.multiple_of((m ^ i[Z]) * wide, wide)
                send[m][...] = through(dy, full[pl.ds(at, wide), :]).astype(BF)
            sums[...] = jnp.zeros_like(sums)
            sums[1:2, :] = jnp.sum(d_a * normed, axis=0, keepdims=True)
            sums[5:6, :] = jnp.sum(d_mid, axis=0, keepdims=True)
            sums[6:7, :] = jnp.sum(d_a, axis=0, keepdims=True)
            sums[7:8, :] = jnp.sum(d_res, axis=0, keepdims=True)

        outs = [shaped((rows, width), F32), shaped((rows, width), BF), shaped((8, width), F32)]
        outs += [shaped((rows, wide), BF)] * n_f
        d_mid, dy, sums, *sends = call(
            second, outs, idx, [d_result, mid, small, full_out, d_own] + got_a,
            flops=2 * rows * width * width,
        )
        got = [both_to(sends[m], lambda i, f: (2 * f + i % 2, m ^ (i // 2))) for m in range(n_f)]
        got += [ctx_to(g, 1) for g in got]

        def down(i, gel, w_ref, own, *send):
            for k in range(n_f):
                part = dot(gel[k * rows : (k + 1) * rows, :], w_ref[...])
                if k:
                    send[k - 1][...] = part.astype(BF)
                else:
                    own[...] = part

        outs = [shaped((rows, width), F32)] + [shaped((rows, width), BF)] * (n_f - 1)
        result, *sends = call(
            down, outs, idx, [gelled, w_down], flops=2 * all_rows * width * hidden
        )
        result = result + mid + small[7]
        for g in send_f(sends):
            result = result + g.astype(F32)

        def attend_back(i, *refs):
            seq_ref, att_ref, lse_ref, refs = refs[0], refs[1], refs[2], refs[3:]
            got, refs = refs[: 2 * n_f], refs[2 * n_f :]
            sum_ref, refs = refs[0], refs[1:]
            send, (kpos, qpos, d_out, d_query, d_keys, d_values) = refs[:n_ctx], refs[n_ctx:]
            fill_positions(i, kpos, qpos)
            for m in range(n_f):
                for swap in range(2):
                    part = got[swap * n_f + m]
                    block = (2 * (m ^ i[FI]) + (i[CORE] ^ swap)) ^ i[CI]
                    at = pl.multiple_of(block * rows, rows)
                    d_out[pl.ds(at, rows), :] = jnp.where(
                        i[CORE] == 0, part[:, :pair], part[:, pair:]
                    )
            d_keys[...] = jnp.zeros_like(d_keys)
            d_values[...] = jnp.zeros_like(d_values)

            def step(e, _):
                here = pl.ds(pl.multiple_of(e * tall, tall), tall)
                allowed = kpos[...] <= qpos[here, :]
                for h in range(heads):
                    cut = slice(h * hd, (h + 1) * hd)
                    query, d_att = seq_ref[here, cut], d_out[here, cut]
                    keys = seq_ref[:, pair + h * hd : pair + (h + 1) * hd]
                    values = seq_ref[:, 2 * pair + h * hd : 2 * pair + (h + 1) * hd]
                    lse = lse_ref[here, h * hd : h * hd + 1]
                    scores = jnp.where(allowed, through(query, keys), -1e30)
                    probs = jnp.exp(scores - lse)
                    delta = jnp.sum(
                        d_att.astype(F32) * att_ref[here, cut].astype(F32), axis=1, keepdims=True
                    )
                    d_scores = (probs * (through(d_att, values) - delta)).astype(BF)
                    d_query[here, cut] = dot(d_scores, keys) * SCALE
                    d_keys[:, cut] += outer(d_scores, query)
                    d_values[:, cut] += outer(probs.astype(BF), d_att)
                return 0

            lax.fori_loop(0, length // tall, step, 0)
            for e in range(n_ctx):
                here = slice(e * rows, (e + 1) * rows)
                send[e][:, :pair] = d_query[here, :].astype(BF)
                send[e][:, pair : 2 * pair] = d_keys[here, :].astype(BF)
                send[e][:, 2 * pair :] = d_values[here, :].astype(BF)
            sum_ref[...] = jnp.zeros_like(sum_ref)
            sum_ref[3:4, :] = jnp.sum(d_query[...], axis=0, keepdims=True)
            sum_ref[4:5, :] = jnp.sum(d_values[...], axis=0, keepdims=True)

        outs = [shaped((8, pair), F32)] + [shaped((rows, 3 * pair), BF)] * n_ctx
        qv_sum, *sends = call(
            attend_back, outs, idx, [seq, att, lse] + got,
            places
            + [
                pltpu.VMEM((length, pair), BF),
                pltpu.VMEM((length, pair), F32),
                pltpu.VMEM((length, pair), F32),
                pltpu.VMEM((length, pair), F32),
            ],
            flops=10 * length * length * pair,
        )
        got = [sends[0]] + [ctx_to(sends[e], e) for e in range(1, n_ctx)]

        n_all_dev = n_ctx * n_f
        per = width // n_all_dev

        def grad_out(i, dy_ref, *refs):
            o_refs, (away, keep, held) = refs[: 2 * n_f], refs[2 * n_f :]
            for m in range(n_f):
                for core in range(2):
                    at = pl.multiple_of((2 * (m ^ i[Z]) + core) * pair, pair)
                    held[pl.ds(at, pair), :] = outer(o_part(i, o_refs, core, m), dy_ref[...])
            for b in range(n_z):
                for f in range(n_f):
                    at = (2 * b + i[CORE]) * n_f * per + f * per
                    keep[f, b * per : (b + 1) * per, :] = held[pl.ds(at, per), :]
                    at = (2 * b + 1 - i[CORE]) * n_f * per + f * per
                    away[f, b * per : (b + 1) * per, :] = held[pl.ds(at, per), :].astype(BF)

        dims = (n_f, n_z * per, width)
        away, out_keep = call(
            grad_out, [shaped(dims, BF), shaped(dims, F32)], idx, [dy] + o_parts,
            [pltpu.VMEM((width, width), F32)], flops=2 * rows * width * width,
        )
        away = ctx_to(away, 1)

        def out_first(i, keep, got, own, *send):
            f = i[FI]
            own[...] = keep[f] + got[f].astype(F32)
            for k in range(1, n_f):
                send[k - 1][...] = (keep[f ^ k] + got[f ^ k].astype(F32)).astype(BF)

        outs = [shaped((n_z * per, width), F32)] + [shaped((n_z * per, width), BF)] * (n_f - 1)
        out_own, *sends = call(out_first, outs, idx, [out_keep, away])
        for g in send_f(sends):
            out_own = out_own + g.astype(F32)

        def first(i, *refs):
            got, refs = refs[:n_ctx], refs[n_ctx:]
            n_refs, refs = refs[:n_f], refs[n_f:]
            full, sum_in, refs = refs[0], refs[1], refs[2:]
            proj_ref, sums, own, send, held = refs[0], refs[1], refs[2], refs[3:-1], refs[-1]
            for e in range(n_ctx):
                held[e] = got[e][...]
            gain_sum = jnp.zeros((1, width), F32)
            shift_sum = jnp.zeros((1, width), F32)
            for k in range(n_f):
                here = slice(k * rows, (k + 1) * rows)
                for p in range(2):
                    e = 2 * (i[FI] ^ i[Z] ^ k) + (i[CORE] ^ p)
                    for q in range(3):
                        at = q * wide + p * pair
                        proj_ref[here, at : at + pair] = held[e, :, q * pair : (q + 1) * pair]
                part = through(proj_ref[here, :], full[...])
                gain_sum += jnp.sum(part * n_refs[k][...].astype(F32), axis=0, keepdims=True)
                shift_sum += jnp.sum(part, axis=0, keepdims=True)
                if k:
                    send[k - 1][...] = part.astype(BF)
                else:
                    own[...] = part
            sums[...] = sum_in[...]
            sums[0:1, :] = gain_sum
            sums[2:3, :] = shift_sum

        outs = [
            shaped((all_rows, 3 * wide), BF),
            shaped((8, width), F32),
            shaped((rows, width), F32),
        ] + [shaped((rows, width), BF)] * (n_f - 1)
        d_proj, sums, d_own, *sends = call(
            first, outs, idx, got + n_all + [full_qkv, sums],
            [pltpu.VMEM((n_ctx, rows, 3 * pair), BF)],
            flops=6 * all_rows * width * wide,
        )
        got_x = send_f(sends)

        block = width // n_ctx
        per_up = hidden // n_ctx

        def pack(i, a_ref, p_ref, sums_ref, up_ref, qv_ref, away, keep, held):
            f, core = i[FI], i[CORE]
            for zz in range(n_z):
                at = slice(2 * zz * block, 2 * (zz + 1) * block)
                held[...] = outer(a_ref[:, at], p_ref[...])
                both = sums_ref[:, at]
                for par, out in ((core, keep), (1 - core, away)):
                    row = pl.ds(pl.multiple_of(par * block, block), block)
                    out[zz, :block, :] = held[row, :].astype(out.dtype)
                    out[zz, block:, :] = jnp.zeros((16, 3 * wide), out.dtype)
                    hit = jnp.logical_and(zz == f, par == core)
                    small = jnp.where(par == 0, both[:, :block], both[:, block:])
                    small = small + jnp.where(hit, qv_ref[...], 0.0)
                    ups = up_ref[:, pl.ds(pl.multiple_of(par * n_f * per_up, n_f * per_up), n_f * per_up)]
                    ups = jnp.where(zz == f, ups, 0.0)
                    out[zz, block : block + 8, :block] = small.astype(out.dtype)
                    for g in range(n_f):
                        out[zz, block + 8 + g : block + 9 + g, :per_up] = ups[
                            :, g * per_up : (g + 1) * per_up
                        ].astype(out.dtype)

        dims = (n_z, block + 16, 3 * wide)
        away, keep = call(
            pack, [shaped(dims, BF), shaped(dims, F32)], idx,
            [a_all, d_proj, sums, up_sum, qv_sum], [pltpu.VMEM((2 * block, 3 * wide), F32)],
            flops=6 * all_rows * width * wide,
        )
        away = ctx_to(away, 1)

        out_own = out_own.reshape(n_z, per, width)
        part_w = 4 * wide

        def over_core(i, keep_ref, got, o_ref, own, *send):
            def fill(out, at):
                out[:, : 3 * wide] = (keep_ref[at] + got[at].astype(F32)).astype(out.dtype)
                out[block:, 3 * wide :] = jnp.zeros((16, wide), out.dtype)
                for g in range(n_f):
                    piece = o_ref[at, :, g * wide : (g + 1) * wide]
                    out[g * per : (g + 1) * per, 3 * wide :] = piece.astype(out.dtype)

            fill(own, i[Z])
            for m in range(1, n_z):
                fill(send[m - 1], i[Z] ^ m)

        dims = (block + 16, part_w)
        outs = [shaped(dims, F32)] + [shaped(dims, BF)] * (n_z - 1)
        own, *sends = call(over_core, outs, idx, [keep, away, out_own])
        got = [ctx_to(s, 2 * (m + 1)) for m, s in enumerate(sends)]
        out_down = both_to(
            part_down, lambda i, f: ((f * n_ctx + i) // n_f, (f * n_ctx + i) % n_f)
        ).astype(F32)

        def over_z(i, *refs):
            own_ref, got, up_ref, refs = refs[0], refs[1:n_z], refs[n_z], refs[n_z + 1 :]
            out_ref, own, send, (held, held_up) = refs[0], refs[1], refs[2:-2], refs[-2:]
            total = own_ref[...]
            for g in got:
                total = total + g[...].astype(F32)
            held[...] = total
            held_up[...] = up_ref[...].astype(F32)
            for g in range(n_f):
                out_ref[:, g * wide : (g + 1) * wide] = total[g * per : (g + 1) * per, 3 * wide :]
            for k in range(n_f):
                at = pl.ds(pl.multiple_of((i[FI] ^ k) * per, per), per)
                out = send[k - 1] if k else own
                out[:per, : 3 * wide] = held[at, : 3 * wide].astype(out.dtype)
                out[:per, 3 * wide :] = held_up[at, :].astype(out.dtype)
                out[per:, :] = jnp.zeros((16, 3 * wide + hidden), out.dtype)
                out[per:, : 3 * wide] = held[block:, : 3 * wide].astype(out.dtype)

        dims = (per + 16, 3 * wide + hidden)
        outs = [shaped((per, width), F32), shaped(dims, F32)] + [shaped(dims, BF)] * (n_f - 1)
        out_out, own, *sends = call(
            over_z, outs, idx, [own] + got + [part_up],
            [pltpu.VMEM((block + 16, part_w), F32), pltpu.VMEM((block, hidden), F32)],
        )
        got = send_f(sends)

        def last(i, own_ref, *refs):
            got, (out, up, small_ref) = refs[: n_f - 1], refs[n_f - 1 :]
            total = own_ref[per:, :block]
            for k in range(n_f):
                src = got[k - 1] if k else own_ref
                for q in range(3):
                    at = pl.ds(pl.multiple_of(q * width + (i[FI] ^ k) * wide, wide), wide)
                    out[:, at] = src[:per, q * wide : (q + 1) * wide].astype(F32)
                at = pl.ds(pl.multiple_of((i[FI] ^ k) * hidden, hidden), hidden)
                up[:, at] = src[:per, 3 * wide :].astype(F32)
                if k:
                    total = total + src[per:, :block].astype(F32)
            small_ref[...] = total

        outs = [shaped((per, 3 * width), F32), shaped((per, n_f * hidden), F32)]
        outs += [shaped((16, block), F32)]
        out_qkv, out_up, tile = call(last, outs, idx, [own] + got)
        out_small = lax.dynamic_slice(tile, (0, fi * per), (8, per))
        out_upb = lax.dynamic_slice(tile, (8 + fi, 0), (1, per_up))

        normed, inv = normalize(x)
        d_a = d_own
        for g in got_x:
            d_a = d_a + g.astype(F32)
        d_input = d_mid + norm_back(d_a * small[0], normed, inv)

        shape = (seqs, slots, blk, width)
        return (
            result.reshape(shape),
            d_input.reshape(shape),
            out_qkv[None],
            out_out[None],
            out_up[None],
            out_down[None],
            out_small[:2][None],
            out_small[2:][None],
            out_upb.reshape(1, -1),
        )

    return layer


def solution(mesh):
    return jax.shard_map(
        build(mesh),
        mesh=mesh,
        in_specs=(
            P("fsdp", "ctx", None, None),
            P(),
            P(None, "fsdp", None),
            P(None, "fsdp", None),
            P(None, "fsdp", None),
            P(None, "fsdp", None),
            P(None, None, "fsdp"),
            P(None, None, "fsdp"),
            P(None, "fsdp"),
            P("fsdp", "ctx", None, None),
        ),
        out_specs=(
            P("fsdp", "ctx", None, None),
            P("fsdp", "ctx", None, None),
            P(None, ("ctx", "fsdp"), None),
            P(None, ("ctx", "fsdp"), None),
            P(None, ("ctx", "fsdp"), None),
            P(None, ("ctx", "fsdp"), None),
            P(None, None, ("ctx", "fsdp")),
            P(None, None, ("ctx", "fsdp")),
            P(None, ("ctx", "fsdp")),
        ),
        check_vma=False,
    )
```

```python
import jax
import jax.numpy as jnp
from jax import lax
from jax.experimental import pallas as pl
from jax.experimental.pallas import tpu as pltpu
from jax.sharding import PartitionSpec as P


HEADS = 16
EPS = 1e-05
SCALE = 0.125
GELU_C = 0.7978845608028654
BF = jnp.bfloat16
F32 = jnp.float32


CI, FI, Z, CORE, ORDER = 0, 1, 2, 3, 8


def normalize(x):
    centred = x - jnp.mean(x, axis=1, keepdims=True)
    inv = lax.rsqrt(jnp.mean(centred * centred, axis=1, keepdims=True) + EPS)
    return (centred * inv, inv)


def norm_back(grad, normed, inv):
    return inv * (
        grad
        - jnp.mean(grad, axis=1, keepdims=True)
        - normed * jnp.mean(grad * normed, axis=1, keepdims=True)
    )


def gelu_parts(u):
    inner = GELU_C * (u + 0.044715 * u * u * u)
    tanhed = jnp.tanh(inner)
    value = 0.5 * u * (1.0 + tanhed)
    slope = 0.5 * (1.0 + tanhed) + 0.5 * u * (1.0 - tanhed * tanhed) * GELU_C * (
        1.0 + 3.0 * 0.044715 * u * u
    )
    return (value, slope)


def dot(a, b):
    return jnp.dot(a, b, preferred_element_type=F32)


def outer(left, right):
    return lax.dot_general(left, right, (((0,), (0,)), ((), ())), preferred_element_type=F32)


def through(left, weight):
    return lax.dot_general(left, weight, (((1,), (1,)), ((), ())), preferred_element_type=F32)


def shaped(shape, kind):
    return jax.ShapeDtypeStruct(shape, kind)


def total_bytes(arrays):
    return sum(a.size * a.dtype.itemsize for a in arrays)


def call(kernel, outs, idx, ins, scratch=(), flops=0, mib=20):
    vmem = pl.BlockSpec(memory_space=pltpu.VMEM)
    return pl.pallas_call(
        kernel,
        out_shape=outs,
        in_specs=[pl.BlockSpec(memory_space=pltpu.SMEM)] + [vmem] * len(ins),
        out_specs=[vmem] * len(outs),
        scratch_shapes=list(scratch),
        compiler_params=pltpu.CompilerParams(vmem_limit_bytes=mib * 1024 * 1024),
        cost_estimate=pl.CostEstimate(
            flops=flops, bytes_accessed=total_bytes(ins) + total_bytes(outs), transcendentals=0
        ),
    )(idx, *ins)


def build(mesh):
    n_ctx, n_f = mesh.shape["ctx"], mesh.shape["fsdp"]
    n_z = n_ctx // 2

    def fsdp_to(x, k):
        return lax.ppermute(x, "fsdp", [(f, f ^ k) for f in range(n_f)])

    def ctx_to(x, e):
        return lax.ppermute(x, "ctx", [(i, i ^ e) for i in range(n_ctx)])

    def both_to(x, target):
        pairs = []
        for i in range(n_ctx):
            for f in range(n_f):
                to_i, to_f = target(i, f)
                pairs.append((i * n_f + f, to_i * n_f + to_f))
        return lax.ppermute(x, ("ctx", "fsdp"), pairs)

    def gather_f(block):
        return [block] + [fsdp_to(block, k) for k in range(1, n_f)]

    def send_f(blocks):
        return [fsdp_to(b, k + 1) for k, b in enumerate(blocks)]

    def share_core(blocks):
        return [ctx_to(b, 1) for b in blocks]

    def fill_rows(full, own, got, other, fi, core, cut=slice(None)):
        depth = own.shape[0]
        half = depth // 2
        full[pl.ds(fi * depth, depth), :] = own[:, cut]
        for k in range(1, n_f):
            base = (fi ^ k) * depth
            full[pl.ds(base + core * half, half), :] = got[k - 1][:half, cut]
            full[pl.ds(base + (1 - core) * half, half), :] = other[k - 1][:half, cut]

    def layer(inputs, block_order, w_qkv, w_out, w_up, w_down, gains, biases, up_bias, out_grad):
        seqs, slots, blk, width = inputs.shape
        rows = seqs * slots * blk
        ci = lax.axis_index("ctx")
        fi = lax.axis_index("fsdp")
        z, c = ci // 2, ci % 2
        mine = 2 * fi + c
        wide = width // n_f
        pair = wide // 2
        hidden = up_bias.shape[1]
        hd = width // HEADS
        heads = pair // hd
        length = n_ctx * rows
        half = wide // 2
        all_rows = n_f * rows
        x = inputs.reshape(rows, width)
        d_result = out_grad.reshape(rows, width)
        w_qkv, w_out, w_up, w_down = w_qkv[0], w_out[0], w_up[0], w_down[0]
        zero = jnp.zeros((), jnp.int32)
        idx = jnp.concatenate(
            [jnp.stack([ci, fi, z, c, mine, zero, zero, zero]).astype(jnp.int32), block_order]
        )
        own_small = jnp.concatenate([gains[0], biases[0]])
        n_small = own_small.shape[0]

        def prep(i, x_ref, w_ref, s_ref, n_ref, own_ref, *send):
            normed, _ = normalize(x_ref[...])
            n_ref[...] = normed.astype(BF)
            f, core = i[FI], i[CORE]
            for q in range(3):
                to = slice(q * wide, (q + 1) * wide)
                at = pl.multiple_of(q * width + f * wide, wide)
                own_ref[:, to] = w_ref[:, pl.ds(at, wide)]
                for k in range(1, n_f):
                    at = pl.multiple_of(q * width + (f ^ k) * wide, wide)
                    row = pl.multiple_of(core * half, half)
                    send[k - 1][:half, to] = w_ref[pl.ds(row, half), pl.ds(at, wide)]
            for k in range(1, n_f):
                send[k - 1][half : half + n_small, :wide] = s_ref[...]

        outs = [shaped((rows, width), BF), shaped((wide, 3 * wide), BF)]
        outs += [shaped((half + 16, 3 * wide), BF)] * (n_f - 1)
        n_one, own_qkv, *sends = call(prep, outs, idx, [x, w_qkv, own_small])
        got_qkv = send_f(sends)
        other_qkv = share_core(got_qkv)
        n_all = gather_f(n_one)

        def project(i, *refs):
            n_refs, refs = refs[:n_f], refs[n_f:]
            own, s_ref, refs = refs[0], refs[1], refs[2:]
            got, refs = refs[: n_f - 1], refs[n_f - 1 :]
            other, refs = refs[: n_f - 1], refs[n_f - 1 :]
            a_ref, full, small, refs = refs[0], refs[1], refs[2], refs[3:]
            send, held = refs[:n_ctx], refs[n_ctx]
            f, core = i[FI], i[CORE]
            for k in range(n_f):
                piece = s_ref[...] if k == 0 else got[k - 1][half : half + n_small, :wide]
                small[:, pl.ds(pl.multiple_of((f ^ k) * wide, wide), wide)] = piece.astype(F32)
            fill_rows(full, own, got, other, f, core)
            at = pl.ds(pl.multiple_of(f * wide, wide), wide)
            q_shift, v_shift = small[3:4, at], small[4:5, at]
            for k in range(n_f):
                a_one = (n_refs[k][...].astype(F32) * small[0:1, :] + small[2:3, :]).astype(BF)
                a_ref[k * rows : (k + 1) * rows, :] = a_one
                proj = dot(a_one, full[...])
                query = ((proj[:, :wide] + q_shift) * SCALE).astype(BF)
                keys = proj[:, wide : 2 * wide].astype(BF)
                values = (proj[:, 2 * wide :] + v_shift).astype(BF)
                for p in range(2):
                    cut = slice(p * pair, (p + 1) * pair)
                    for q, part in enumerate((query, keys, values)):
                        held[k, p, :, q * pair : (q + 1) * pair] = part[:, cut]
            for e in range(n_ctx):
                send[e][...] = held[i[FI] ^ i[Z] ^ (e >> 1), core ^ (e & 1)]

        outs = [
            shaped((all_rows, width), BF),
            shaped((width, 3 * wide), BF),
            shaped((n_small, width), F32),
        ] + [shaped((rows, 3 * pair), BF)] * n_ctx
        a_all, full_qkv, small, *sends = call(
            project, outs, idx,
            n_all + [own_qkv, own_small] + got_qkv + other_qkv,
            [pltpu.VMEM((n_f, 2, rows, 3 * pair), BF)],
            flops=6 * all_rows * width * wide,
        )
        got = [sends[0]] + [ctx_to(sends[e], e) for e in range(1, n_ctx)]

        def cut_weights(i, up_ref, out_ref, own_ref, *send):
            f, core = i[FI], i[CORE]
            row = pl.ds(pl.multiple_of(core * half, half), half)
            own_ref[:, :hidden] = up_ref[:, pl.ds(pl.multiple_of(f * hidden, hidden), hidden)]
            own_ref[:, hidden:] = out_ref[...]
            for k in range(1, n_f):
                at = pl.ds(pl.multiple_of((f ^ k) * hidden, hidden), hidden)
                send[k - 1][:, :hidden] = up_ref[row, at]
                send[k - 1][:, hidden:] = out_ref[row, :]

        outs = [shaped((wide, hidden + width), BF)]
        outs += [shaped((half, hidden + width), BF)] * (n_f - 1)
        own_w, *sends = call(cut_weights, outs, idx, [w_up, w_out])
        got_w = send_f(sends)
        other_w = share_core(got_w)
        dz, _ = lax.optimization_barrier((d_result.astype(BF), n_all))
        dz_all = lax.all_gather(dz, "fsdp", axis=0, tiled=True)

        def positions(i, block, along):
            dims = (rows, 1) if along == 0 else (1, rows)
            at = lax.broadcasted_iota(jnp.int32, dims, along)
            pos = at + i[ORDER + block * slots] * blk
            for s in range(1, slots):
                moved = at - s * blk + i[ORDER + block * slots + s] * blk
                pos = jnp.where(at >= s * blk, moved, pos)
            return pos

        def fill_positions(i, kpos, qpos):
            for e in range(n_ctx):
                here = slice(e * rows, (e + 1) * rows)
                kpos[:, here] = positions(i, i[CI] ^ e, 1)
                qpos[here, :] = positions(i, i[CI] ^ e, 0)

        tall = 2 * rows
        places = [pltpu.VMEM((1, length), jnp.int32), pltpu.VMEM((length, 1), jnp.int32)]

        def attend(i, *refs):
            got, refs = refs[:n_ctx], refs[n_ctx:]
            seq, att, lse_ref, refs = refs[0], refs[1], refs[2], refs[3:]
            send, (kpos, qpos) = refs[:n_f], refs[n_f:]
            for e in range(n_ctx):
                seq[e * rows : (e + 1) * rows, :] = got[e][...]
            fill_positions(i, kpos, qpos)

            def step(e, _):
                here = pl.ds(pl.multiple_of(e * tall, tall), tall)
                allowed = kpos[...] <= qpos[here, :]
                for h in range(heads):
                    cut = slice(h * hd, (h + 1) * hd)
                    keys = seq[:, pair + h * hd : pair + (h + 1) * hd]
                    values = seq[:, 2 * pair + h * hd : 2 * pair + (h + 1) * hd]
                    scores = jnp.where(allowed, through(seq[here, cut], keys), -1e30)
                    top = jnp.max(scores, axis=1, keepdims=True)
                    probs = jnp.exp(scores - top)
                    norm = jnp.sum(probs, axis=1, keepdims=True)
                    out = dot(probs.astype(BF), values) / norm
                    att[here, cut] = out.astype(BF)
                    lse_ref[here, cut] = jnp.broadcast_to(top + jnp.log(norm), (tall, hd))
                return 0

            lax.fori_loop(0, length // tall, step, 0)
            for m in range(n_f):
                for core in range(2):
                    block = (2 * (m ^ i[FI]) + core) ^ i[CI]
                    at = pl.multiple_of(block * rows, rows)
                    send[m][core * rows : (core + 1) * rows, :] = att[pl.ds(at, rows), :]

        outs = [shaped((length, 3 * pair), BF), shaped((length, pair), BF), shaped((length, pair), F32)]
        outs += [shaped((tall, pair), BF)] * n_f
        seq, att, lse, *sends = call(
            attend, outs, idx, got, places, flops=4 * length * length * pair
        )
        got = [both_to(sends[m], lambda i, f: (2 * (m ^ f) + i % 2, i // 2)) for m in range(n_f)]
        o_parts = got + [ctx_to(g, 1) for g in got]

        def o_part(i, refs, core, m):
            here = pl.ds(pl.multiple_of(i[CORE] * rows, rows), rows)
            own, other = refs[m][here, :], refs[n_f + m][here, :]
            return jnp.where(core == i[CORE], own, other)

        def finish(i, *refs):
            x_ref, small_ref, refs = refs[0], refs[1], refs[2:]
            o_refs, refs = refs[: 2 * n_f], refs[2 * n_f :]
            own, refs = refs[0], refs[1:]
            got_o, refs = refs[: n_f - 1], refs[n_f - 1 :]
            other_o, refs = refs[: n_f - 1], refs[n_f - 1 :]
            mid_ref, a_ref, full = refs
            fill_rows(full, own, got_o, other_o, i[FI], i[CORE], slice(hidden, None))
            mid = x_ref[...] + small_ref[5:6, :]
            for m in range(n_f):
                for core in range(2):
                    at = pl.multiple_of((2 * (m ^ i[Z]) + core) * pair, pair)
                    mid = mid + dot(o_part(i, o_refs, core, m), full[pl.ds(at, pair), :])
            mid_ref[...] = mid
            normed, _ = normalize(mid)
            a_ref[...] = (normed * small_ref[1:2, :] + small_ref[6:7, :]).astype(BF)

        outs = [shaped((rows, width), F32), shaped((rows, width), BF), shaped((width, width), BF)]
        mid, a_two, full_out = call(
            finish, outs, idx,
            [x, small] + o_parts + [own_w] + got_w + other_w,
            flops=2 * rows * width * width,
        )
        a2_parts = gather_f(a_two)

        def forward(i, *refs):
            a_refs, refs = refs[:n_f], refs[n_f:]
            own_w_ref, bias, refs = refs[0], refs[1], refs[2:]
            got_u, other_u = refs[: n_f - 1], refs[n_f - 1 : 2 * n_f - 2]
            up, a_ref, gel, slope_ref = refs[2 * n_f - 2 :]
            fill_rows(up, own_w_ref, got_u, other_u, i[FI], i[CORE], slice(0, hidden))
            for k in range(n_f):
                here = pl.ds(pl.multiple_of((i[FI] ^ k) * rows, rows), rows)
                a_two = a_refs[k][...]
                a_ref[here, :] = a_two
                value, slope = gelu_parts(dot(a_two, up[...]) + bias[...].astype(F32))
                gel[here, :] = value.astype(BF)
                slope_ref[here, :] = slope.astype(BF)

        outs = [
            shaped((width, hidden), BF),
            shaped((all_rows, width), BF),
            shaped((all_rows, hidden), BF),
            shaped((all_rows, hidden), BF),
        ]
        full_up, a2_all, gelled, slope = call(
            forward, outs, idx, a2_parts + [own_w, up_bias] + got_w + other_w,
            flops=2 * all_rows * width * hidden, mib=54,
        )
        g_down = outer(gelled, dz_all).astype(BF)

        def scatter_ctx(g):
            return lax.psum_scatter(g, "ctx", scatter_dimension=0, tiled=True)

        part_down = scatter_ctx(g_down)

        def backward(i, dz_ref, slope_ref, down, up, du_ref, sum_ref, own, *send):
            total = jnp.zeros((1, hidden), F32)
            for k in range(n_f):
                here = pl.ds(pl.multiple_of((i[FI] ^ k) * rows, rows), rows)
                d_pre = through(dz_ref[here, :], down[...]) * slope_ref[here, :].astype(F32)
                total = total + jnp.sum(d_pre, axis=0, keepdims=True)
                d_hidden = d_pre.astype(BF)
                du_ref[here, :] = d_hidden
                part = through(d_hidden, up[...])
                if k:
                    send[k - 1][...] = part.astype(BF)
                else:
                    own[...] = part
            sum_ref[...] = total

        outs = [
            shaped((all_rows, hidden), BF),
            shaped((1, hidden), F32),
            shaped((rows, width), F32),
        ] + [shaped((rows, width), BF)] * (n_f - 1)
        d_hidden, up_sum, d_own, *sends = call(
            backward, outs, idx, [dz_all, slope, w_down, full_up],
            flops=4 * all_rows * width * hidden, mib=54,
        )
        got_a = send_f(sends)
        g_up = outer(a2_all, d_hidden).astype(BF)

        part_up = scatter_ctx(g_up)

        def second(i, *refs):
            d_ref, mid_ref, small_ref, full, own, refs = (*refs[:5], refs[5:])
            got, refs = refs[: n_f - 1], refs[n_f - 1 :]
            dmid_ref, dy_ref, sums, send = refs[0], refs[1], refs[2], refs[3:]
            d_a = own[...]
            for g in got:
                d_a = d_a + g[...].astype(F32)
            normed, inv = normalize(mid_ref[...])
            d_res = d_ref[...]
            d_mid = d_res + norm_back(d_a * small_ref[1:2, :], normed, inv)
            dmid_ref[...] = d_mid
            dy = d_mid.astype(BF)
            dy_ref[...] = dy
            for m in range(n_f):
                at = pl.multiple_of((m ^ i[Z]) * wide, wide)
                send[m][...] = through(dy, full[pl.ds(at, wide), :]).astype(BF)
            sums[...] = jnp.zeros_like(sums)
            sums[1:2, :] = jnp.sum(d_a * normed, axis=0, keepdims=True)
            sums[5:6, :] = jnp.sum(d_mid, axis=0, keepdims=True)
            sums[6:7, :] = jnp.sum(d_a, axis=0, keepdims=True)
            sums[7:8, :] = jnp.sum(d_res, axis=0, keepdims=True)

        outs = [shaped((rows, width), F32), shaped((rows, width), BF), shaped((8, width), F32)]
        outs += [shaped((rows, wide), BF)] * n_f
        d_mid, dy, sums, *sends = call(
            second, outs, idx, [d_result, mid, small, full_out, d_own] + got_a,
            flops=2 * rows * width * width,
        )
        got = [both_to(sends[m], lambda i, f: (2 * f + i % 2, m ^ (i // 2))) for m in range(n_f)]
        got += [ctx_to(g, 1) for g in got]

        def attend_back(i, *refs):
            seq_ref, att_ref, lse_ref, refs = refs[0], refs[1], refs[2], refs[3:]
            got, refs = refs[: 2 * n_f], refs[2 * n_f :]
            sum_ref, refs = refs[0], refs[1:]
            send, (kpos, qpos, d_out, d_query, d_keys, d_values) = refs[:n_ctx], refs[n_ctx:]
            fill_positions(i, kpos, qpos)
            for m in range(n_f):
                for swap in range(2):
                    part = got[swap * n_f + m]
                    block = (2 * (m ^ i[FI]) + (i[CORE] ^ swap)) ^ i[CI]
                    at = pl.multiple_of(block * rows, rows)
                    d_out[pl.ds(at, rows), :] = jnp.where(
                        i[CORE] == 0, part[:, :pair], part[:, pair:]
                    )
            d_keys[...] = jnp.zeros_like(d_keys)
            d_values[...] = jnp.zeros_like(d_values)

            def step(e, _):
                here = pl.ds(pl.multiple_of(e * tall, tall), tall)
                allowed = kpos[...] <= qpos[here, :]
                for h in range(heads):
                    cut = slice(h * hd, (h + 1) * hd)
                    query, d_att = seq_ref[here, cut], d_out[here, cut]
                    keys = seq_ref[:, pair + h * hd : pair + (h + 1) * hd]
                    values = seq_ref[:, 2 * pair + h * hd : 2 * pair + (h + 1) * hd]
                    lse = lse_ref[here, h * hd : h * hd + 1]
                    scores = jnp.where(allowed, through(query, keys), -1e30)
                    probs = jnp.exp(scores - lse)
                    delta = jnp.sum(
                        d_att.astype(F32) * att_ref[here, cut].astype(F32), axis=1, keepdims=True
                    )
                    d_scores = (probs * (through(d_att, values) - delta)).astype(BF)
                    d_query[here, cut] = dot(d_scores, keys) * SCALE
                    d_keys[:, cut] += outer(d_scores, query)
                    d_values[:, cut] += outer(probs.astype(BF), d_att)
                return 0

            lax.fori_loop(0, length // tall, step, 0)
            for e in range(n_ctx):
                here = slice(e * rows, (e + 1) * rows)
                send[e][:, :pair] = d_query[here, :].astype(BF)
                send[e][:, pair : 2 * pair] = d_keys[here, :].astype(BF)
                send[e][:, 2 * pair :] = d_values[here, :].astype(BF)
            sum_ref[...] = jnp.zeros_like(sum_ref)
            sum_ref[3:4, :] = jnp.sum(d_query[...], axis=0, keepdims=True)
            sum_ref[4:5, :] = jnp.sum(d_values[...], axis=0, keepdims=True)

        outs = [shaped((8, pair), F32)] + [shaped((rows, 3 * pair), BF)] * n_ctx
        qv_sum, *sends = call(
            attend_back, outs, idx, [seq, att, lse] + got,
            places
            + [
                pltpu.VMEM((length, pair), BF),
                pltpu.VMEM((length, pair), F32),
                pltpu.VMEM((length, pair), F32),
                pltpu.VMEM((length, pair), F32),
            ],
            flops=10 * length * length * pair,
        )
        got = [sends[0]] + [ctx_to(sends[e], e) for e in range(1, n_ctx)]

        n_all_dev = n_ctx * n_f
        per = width // n_all_dev

        def grad_out(i, dy_ref, *refs):
            o_refs, (away, keep, held) = refs[: 2 * n_f], refs[2 * n_f :]
            for m in range(n_f):
                for core in range(2):
                    at = pl.multiple_of((2 * (m ^ i[Z]) + core) * pair, pair)
                    held[pl.ds(at, pair), :] = outer(o_part(i, o_refs, core, m), dy_ref[...])
            for b in range(n_z):
                for f in range(n_f):
                    at = (2 * b + i[CORE]) * n_f * per + f * per
                    keep[f, b * per : (b + 1) * per, :] = held[pl.ds(at, per), :]
                    at = (2 * b + 1 - i[CORE]) * n_f * per + f * per
                    away[f, b * per : (b + 1) * per, :] = held[pl.ds(at, per), :].astype(BF)

        dims = (n_f, n_z * per, width)
        away, out_keep = call(
            grad_out, [shaped(dims, BF), shaped(dims, F32)], idx, [dy] + o_parts,
            [pltpu.VMEM((width, width), F32)], flops=2 * rows * width * width,
        )
        away = ctx_to(away, 1)

        def out_first(i, keep, got, own, *send):
            f = i[FI]
            own[...] = keep[f] + got[f].astype(F32)
            for k in range(1, n_f):
                send[k - 1][...] = (keep[f ^ k] + got[f ^ k].astype(F32)).astype(BF)

        outs = [shaped((n_z * per, width), F32)] + [shaped((n_z * per, width), BF)] * (n_f - 1)
        out_own, *sends = call(out_first, outs, idx, [out_keep, away])
        out_got = send_f(sends)

        def out_second(i, own_ref, *refs):
            got, (own, *send), held = refs[: n_f - 1], refs[n_f - 1 : -1], refs[-1]
            total = own_ref[...]
            for g in got:
                total = total + g[...].astype(F32)
            held[...] = total
            own[...] = held[pl.ds(pl.multiple_of(i[Z] * per, per), per), :]
            for m in range(1, n_z):
                at = pl.ds(pl.multiple_of((i[Z] ^ m) * per, per), per)
                send[m - 1][...] = held[at, :].astype(BF)

        outs = [shaped((per, width), F32)] + [shaped((per, width), BF)] * (n_z - 1)
        out_own, *sends = call(
            out_second, outs, idx, [out_own] + out_got,
            [pltpu.VMEM((n_z * per, width), F32)],
        )
        out_got = [ctx_to(s, 2 * (m + 1)) for m, s in enumerate(sends)]

        def first(i, *refs):
            got, refs = refs[:n_ctx], refs[n_ctx:]
            n_refs, refs = refs[:n_f], refs[n_f:]
            full, sum_in, refs = refs[0], refs[1], refs[2:]
            proj_ref, sums, own, send, held = refs[0], refs[1], refs[2], refs[3:-1], refs[-1]
            for e in range(n_ctx):
                held[e] = got[e][...]
            gain_sum = jnp.zeros((1, width), F32)
            shift_sum = jnp.zeros((1, width), F32)
            for k in range(n_f):
                here = slice(k * rows, (k + 1) * rows)
                for p in range(2):
                    e = 2 * (i[FI] ^ i[Z] ^ k) + (i[CORE] ^ p)
                    for q in range(3):
                        at = q * wide + p * pair
                        proj_ref[here, at : at + pair] = held[e, :, q * pair : (q + 1) * pair]
                part = through(proj_ref[here, :], full[...])
                gain_sum += jnp.sum(part * n_refs[k][...].astype(F32), axis=0, keepdims=True)
                shift_sum += jnp.sum(part, axis=0, keepdims=True)
                if k:
                    send[k - 1][...] = part.astype(BF)
                else:
                    own[...] = part
            sums[...] = sum_in[...]
            sums[0:1, :] = gain_sum
            sums[2:3, :] = shift_sum

        outs = [
            shaped((all_rows, 3 * wide), BF),
            shaped((8, width), F32),
            shaped((rows, width), F32),
        ] + [shaped((rows, width), BF)] * (n_f - 1)
        d_proj, sums, d_own, *sends = call(
            first, outs, idx, got + n_all + [full_qkv, sums],
            [pltpu.VMEM((n_ctx, rows, 3 * pair), BF)],
            flops=6 * all_rows * width * wide, mib=54,
        )
        got_x = send_f(sends)

        block = width // n_ctx
        per_up = hidden // n_ctx

        def pack(i, a_ref, p_ref, sums_ref, up_ref, qv_ref, away, keep, held):
            f, core = i[FI], i[CORE]
            for zz in range(n_z):
                at = slice(2 * zz * block, 2 * (zz + 1) * block)
                held[...] = outer(a_ref[:, at], p_ref[...])
                both = sums_ref[:, at]
                for par, out in ((core, keep), (1 - core, away)):
                    row = pl.ds(pl.multiple_of(par * block, block), block)
                    out[zz, :block, :] = held[row, :].astype(out.dtype)
                    out[zz, block:, :] = jnp.zeros((16, 3 * wide), out.dtype)
                    hit = jnp.logical_and(zz == f, par == core)
                    small = jnp.where(par == 0, both[:, :block], both[:, block:])
                    small = small + jnp.where(hit, qv_ref[...], 0.0)
                    ups = up_ref[:, pl.ds(pl.multiple_of(par * n_f * per_up, n_f * per_up), n_f * per_up)]
                    ups = jnp.where(zz == f, ups, 0.0)
                    out[zz, block : block + 8, :block] = small.astype(out.dtype)
                    for g in range(n_f):
                        out[zz, block + 8 + g : block + 9 + g, :per_up] = ups[
                            :, g * per_up : (g + 1) * per_up
                        ].astype(out.dtype)

        dims = (n_z, block + 16, 3 * wide)
        away, keep = call(
            pack, [shaped(dims, BF), shaped(dims, F32)], idx,
            [a_all, d_proj, sums, up_sum, qv_sum], [pltpu.VMEM((2 * block, 3 * wide), F32)],
            flops=6 * all_rows * width * wide,
        )
        away = ctx_to(away, 1)

        def over_core(i, keep_ref, got, own, *send):
            own[...] = keep_ref[i[Z]] + got[i[Z]].astype(F32)
            for m in range(1, n_z):
                at = i[Z] ^ m
                send[m - 1][...] = (keep_ref[at] + got[at].astype(F32)).astype(BF)

        outs = [shaped(dims[1:], F32)] + [shaped(dims[1:], BF)] * (n_z - 1)
        own, *sends = call(over_core, outs, idx, [keep, away])
        got = [ctx_to(s, 2 * (m + 1)) for m, s in enumerate(sends)]
        low_down = both_to(part_down, lambda i, f: ((f * n_ctx + i) // n_f, (f * n_ctx + i) % n_f))

        def down(i, gel, w_ref, own, *send):
            for k in range(n_f):
                here = pl.ds(pl.multiple_of((i[FI] ^ k) * rows, rows), rows)
                part = dot(gel[here, :], w_ref[...])
                if k:
                    send[k - 1][...] = part.astype(BF)
                else:
                    own[...] = part

        outs = [shaped((rows, width), F32)] + [shaped((rows, width), BF)] * (n_f - 1)
        z_own, *sends = call(down, outs, idx, [gelled, w_down], flops=2 * all_rows * width * hidden)
        z_got = send_f(sends)

        def add_up(i, own, mid_ref, small_ref, *refs):
            total = own[...]
            for g in refs[:-1]:
                total = total + g[...].astype(F32)
            refs[-1][...] = total + mid_ref[...] + small_ref[7:8, :]

        (result,) = call(add_up, [shaped((rows, width), F32)], idx, [z_own, mid, small] + z_got)

        def input_grad(i, x_ref, dmid_ref, small_ref, low_ref, own, *refs):
            got, (out, wider) = refs[:-2], refs[-2:]
            normed, inv = normalize(x_ref[...])
            d_a = own[...]
            for g in got:
                d_a = d_a + g[...].astype(F32)
            out[...] = dmid_ref[...] + norm_back(d_a * small_ref[0:1, :], normed, inv)
            wider[...] = low_ref[...].astype(F32)

        outs = [shaped((rows, width), F32), shaped(low_down.shape, F32)]
        d_input, out_down = call(input_grad, outs, idx, [x, d_mid, small, low_down, d_own] + got_x)

        def over_z(i, *refs):
            own_ref, got, refs = refs[0], refs[1:n_z], refs[n_z:]
            o_ref, got_o, up_ref, refs = refs[0], refs[1:n_z], refs[n_z], refs[n_z + 1 :]
            out_ref, own, send, (held, held_up) = refs[0], refs[1], refs[2:-2], refs[-2:]
            out = o_ref[...]
            for g in got_o:
                out = out + g[...].astype(F32)
            out_ref[...] = out
            total = own_ref[...]
            for g in got:
                total = total + g[...].astype(F32)
            held[...] = total
            held_up[...] = up_ref[...].astype(F32)
            for k in range(n_f):
                at = pl.ds(pl.multiple_of((i[FI] ^ k) * per, per), per)
                out = send[k - 1] if k else own
                out[:per, : 3 * wide] = held[at, : 3 * wide].astype(out.dtype)
                out[:per, 3 * wide :] = held_up[at, :].astype(out.dtype)
                out[per:, :] = jnp.zeros((16, 3 * wide + hidden), out.dtype)
                out[per:, : 3 * wide] = held[block:, : 3 * wide].astype(out.dtype)

        dims = (per + 16, 3 * wide + hidden)
        outs = [shaped((per, width), F32), shaped(dims, F32)] + [shaped(dims, BF)] * (n_f - 1)
        out_out, own, *sends = call(
            over_z, outs, idx, [own] + got + [out_own] + out_got + [part_up],
            [pltpu.VMEM((block + 16, 3 * wide), F32), pltpu.VMEM((block, hidden), F32)],
            mib=54,
        )
        got = send_f(sends)

        def last(i, own_ref, *refs):
            got, (out, up, small_ref, bias_ref) = refs[: n_f - 1], refs[n_f - 1 :]
            total = own_ref[per:, :block]
            for k in range(n_f):
                src = got[k - 1] if k else own_ref
                for q in range(3):
                    at = pl.ds(pl.multiple_of(q * width + (i[FI] ^ k) * wide, wide), wide)
                    out[:, at] = src[:per, q * wide : (q + 1) * wide].astype(F32)
                at = pl.ds(pl.multiple_of((i[FI] ^ k) * hidden, hidden), hidden)
                up[:, at] = src[:per, 3 * wide :].astype(F32)
                if k:
                    total = total + src[per:, :block].astype(F32)
            share, ups = total[:8, :per], total[8:9, :per_up]
            for g in range(1, n_f):
                share = jnp.where(i[FI] == g, total[:8, g * per : (g + 1) * per], share)
                ups = jnp.where(i[FI] == g, total[8 + g : 9 + g, :per_up], ups)
            small_ref[...] = share
            bias_ref[...] = ups

        outs = [shaped((per, 3 * width), F32), shaped((per, n_f * hidden), F32)]
        outs += [shaped((8, per), F32), shaped((1, per_up), F32)]
        out_qkv, out_up, out_small, out_upb = call(last, outs, idx, [own] + got)

        shape = (seqs, slots, blk, width)
        return (
            result.reshape(shape),
            d_input.reshape(shape),
            out_qkv[None],
            out_out[None],
            out_up[None],
            out_down[None],
            out_small[:2][None],
            out_small[2:][None],
            out_upb.reshape(1, -1),
        )

    return layer


def solution(mesh):
    return jax.shard_map(
        build(mesh),
        mesh=mesh,
        in_specs=(
            P("fsdp", "ctx", None, None),
            P(),
            P(None, "fsdp", None),
            P(None, "fsdp", None),
            P(None, "fsdp", None),
            P(None, "fsdp", None),
            P(None, None, "fsdp"),
            P(None, None, "fsdp"),
            P(None, "fsdp"),
            P("fsdp", "ctx", None, None),
        ),
        out_specs=(
            P("fsdp", "ctx", None, None),
            P("fsdp", "ctx", None, None),
            P(None, ("ctx", "fsdp"), None),
            P(None, ("ctx", "fsdp"), None),
            P(None, ("ctx", "fsdp"), None),
            P(None, ("ctx", "fsdp"), None),
            P(None, None, ("ctx", "fsdp")),
            P(None, None, ("ctx", "fsdp")),
            P(None, ("ctx", "fsdp")),
        ),
        check_vma=False,
    )
```

```python
import jax
import jax.numpy as jnp
from jax import lax
from jax.experimental import pallas as pl
from jax.experimental.pallas import tpu as pltpu
from jax.sharding import PartitionSpec as P


HEADS = 16
EPS = 1e-05
SCALE = 0.125
GELU_C = 0.7978845608028654
BF = jnp.bfloat16
F32 = jnp.float32


CI, FI, Z, CORE, ORDER = 0, 1, 2, 3, 8


def normalize(x):
    centred = x - jnp.mean(x, axis=1, keepdims=True)
    inv = lax.rsqrt(jnp.mean(centred * centred, axis=1, keepdims=True) + EPS)
    return (centred * inv, inv)


def norm_back(grad, normed, inv):
    return inv * (
        grad
        - jnp.mean(grad, axis=1, keepdims=True)
        - normed * jnp.mean(grad * normed, axis=1, keepdims=True)
    )


def gelu_parts(u):
    inner = GELU_C * (u + 0.044715 * u * u * u)
    tanhed = jnp.tanh(inner)
    value = 0.5 * u * (1.0 + tanhed)
    slope = 0.5 * (1.0 + tanhed) + 0.5 * u * (1.0 - tanhed * tanhed) * GELU_C * (
        1.0 + 3.0 * 0.044715 * u * u
    )
    return (value, slope)


def dot(a, b):
    return jnp.dot(a, b, preferred_element_type=F32)


def outer(left, right):
    return lax.dot_general(left, right, (((0,), (0,)), ((), ())), preferred_element_type=F32)


def through(left, weight):
    return lax.dot_general(left, weight, (((1,), (1,)), ((), ())), preferred_element_type=F32)


def shaped(shape, kind):
    return jax.ShapeDtypeStruct(shape, kind)


def total_bytes(arrays):
    return sum(a.size * a.dtype.itemsize for a in arrays)


def call(kernel, outs, idx, ins, scratch=(), flops=0, mib=20):
    vmem = pl.BlockSpec(memory_space=pltpu.VMEM)
    return pl.pallas_call(
        kernel,
        out_shape=outs,
        in_specs=[pl.BlockSpec(memory_space=pltpu.SMEM)] + [vmem] * len(ins),
        out_specs=[vmem] * len(outs),
        scratch_shapes=list(scratch),
        compiler_params=pltpu.CompilerParams(vmem_limit_bytes=mib * 1024 * 1024),
        cost_estimate=pl.CostEstimate(
            flops=flops, bytes_accessed=total_bytes(ins) + total_bytes(outs), transcendentals=0
        ),
    )(idx, *ins)


def build(mesh):
    n_ctx, n_f = mesh.shape["ctx"], mesh.shape["fsdp"]
    n_z = n_ctx // 2

    def fsdp_to(x, k):
        return lax.ppermute(x, "fsdp", [(f, f ^ k) for f in range(n_f)])

    def ctx_to(x, e):
        return lax.ppermute(x, "ctx", [(i, i ^ e) for i in range(n_ctx)])

    def both_to(x, target):
        pairs = []
        for i in range(n_ctx):
            for f in range(n_f):
                to_i, to_f = target(i, f)
                pairs.append((i * n_f + f, to_i * n_f + to_f))
        return lax.ppermute(x, ("ctx", "fsdp"), pairs)

    def gather_f(block):
        return [block] + [fsdp_to(block, k) for k in range(1, n_f)]

    def send_f(blocks):
        return [fsdp_to(b, k + 1) for k, b in enumerate(blocks)]

    def share_core(blocks):
        return [ctx_to(b, 1) for b in blocks]

    def fill_rows(full, own, got, other, fi, core, cut=slice(None)):
        depth = own.shape[0]
        half = depth // 2
        full[pl.ds(fi * depth, depth), :] = own[:, cut]
        for k in range(1, n_f):
            base = (fi ^ k) * depth
            full[pl.ds(base + core * half, half), :] = got[k - 1][:half, cut]
            full[pl.ds(base + (1 - core) * half, half), :] = other[k - 1][:half, cut]

    def layer(inputs, block_order, w_qkv, w_out, w_up, w_down, gains, biases, up_bias, out_grad):
        seqs, slots, blk, width = inputs.shape
        rows = seqs * slots * blk
        ci = lax.axis_index("ctx")
        fi = lax.axis_index("fsdp")
        z, c = ci // 2, ci % 2
        mine = 2 * fi + c
        wide = width // n_f
        pair = wide // 2
        hidden = up_bias.shape[1]
        hd = width // HEADS
        heads = pair // hd
        length = n_ctx * rows
        half = wide // 2
        all_rows = n_f * rows
        x = inputs.reshape(rows, width)
        d_result = out_grad.reshape(rows, width)
        w_qkv, w_out, w_up, w_down = w_qkv[0], w_out[0], w_up[0], w_down[0]
        zero = jnp.zeros((), jnp.int32)
        idx = jnp.concatenate(
            [jnp.stack([ci, fi, z, c, mine, zero, zero, zero]).astype(jnp.int32), block_order]
        )
        own_small = jnp.concatenate([gains[0], biases[0]])
        n_small = own_small.shape[0]

        def prep(i, x_ref, w_ref, s_ref, n_ref, own_ref, *send):
            normed, _ = normalize(x_ref[...])
            n_ref[...] = normed.astype(BF)
            f, core = i[FI], i[CORE]
            for q in range(3):
                to = slice(q * wide, (q + 1) * wide)
                at = pl.multiple_of(q * width + f * wide, wide)
                own_ref[:, to] = w_ref[:, pl.ds(at, wide)]
                for k in range(1, n_f):
                    at = pl.multiple_of(q * width + (f ^ k) * wide, wide)
                    row = pl.multiple_of(core * half, half)
                    send[k - 1][:half, to] = w_ref[pl.ds(row, half), pl.ds(at, wide)]
            for k in range(1, n_f):
                send[k - 1][half : half + n_small, :wide] = s_ref[...]

        outs = [shaped((rows, width), BF), shaped((wide, 3 * wide), BF)]
        outs += [shaped((half + 16, 3 * wide), BF)] * (n_f - 1)
        n_one, own_qkv, *sends = call(prep, outs, idx, [x, w_qkv, own_small])
        got_qkv = send_f(sends)
        other_qkv = share_core(got_qkv)
        n_all = gather_f(n_one)

        def project(i, *refs):
            n_refs, refs = refs[:n_f], refs[n_f:]
            own, s_ref, refs = refs[0], refs[1], refs[2:]
            got, refs = refs[: n_f - 1], refs[n_f - 1 :]
            other, refs = refs[: n_f - 1], refs[n_f - 1 :]
            a_ref, full, small, refs = refs[0], refs[1], refs[2], refs[3:]
            send, held = refs[:n_ctx], refs[n_ctx]
            f, core = i[FI], i[CORE]
            for k in range(n_f):
                piece = s_ref[...] if k == 0 else got[k - 1][half : half + n_small, :wide]
                small[:, pl.ds(pl.multiple_of((f ^ k) * wide, wide), wide)] = piece.astype(F32)
            fill_rows(full, own, got, other, f, core)
            at = pl.ds(pl.multiple_of(f * wide, wide), wide)
            q_shift, v_shift = small[3:4, at], small[4:5, at]
            for k in range(n_f):
                a_one = (n_refs[k][...].astype(F32) * small[0:1, :] + small[2:3, :]).astype(BF)
                a_ref[k * rows : (k + 1) * rows, :] = a_one
                proj = dot(a_one, full[...])
                query = ((proj[:, :wide] + q_shift) * SCALE).astype(BF)
                keys = proj[:, wide : 2 * wide].astype(BF)
                values = (proj[:, 2 * wide :] + v_shift).astype(BF)
                for p in range(2):
                    cut = slice(p * pair, (p + 1) * pair)
                    for q, part in enumerate((query, keys, values)):
                        held[k, p, :, q * pair : (q + 1) * pair] = part[:, cut]
            for e in range(n_ctx):
                send[e][...] = held[i[FI] ^ i[Z] ^ (e >> 1), core ^ (e & 1)]

        outs = [
            shaped((all_rows, width), BF),
            shaped((width, 3 * wide), BF),
            shaped((n_small, width), F32),
        ] + [shaped((rows, 3 * pair), BF)] * n_ctx
        a_all, full_qkv, small, *sends = call(
            project, outs, idx,
            n_all + [own_qkv, own_small] + got_qkv + other_qkv,
            [pltpu.VMEM((n_f, 2, rows, 3 * pair), BF)],
            flops=6 * all_rows * width * wide,
        )
        got = [sends[0]] + [ctx_to(sends[e], e) for e in range(1, n_ctx)]

        def cut_weights(i, up_ref, out_ref, own_ref, *send):
            f, core = i[FI], i[CORE]
            row = pl.ds(pl.multiple_of(core * half, half), half)
            own_ref[:, :hidden] = up_ref[:, pl.ds(pl.multiple_of(f * hidden, hidden), hidden)]
            own_ref[:, hidden:] = out_ref[...]
            for k in range(1, n_f):
                at = pl.ds(pl.multiple_of((f ^ k) * hidden, hidden), hidden)
                send[k - 1][:, :hidden] = up_ref[row, at]
                send[k - 1][:, hidden:] = out_ref[row, :]

        outs = [shaped((wide, hidden + width), BF)]
        outs += [shaped((half, hidden + width), BF)] * (n_f - 1)
        own_w, *sends = call(cut_weights, outs, idx, [w_up, w_out])
        got_w = send_f(sends)
        other_w = share_core(got_w)
        dz, _ = lax.optimization_barrier((d_result.astype(BF), n_all))
        dz_all = lax.all_gather(dz, "fsdp", axis=0, tiled=True)

        def positions(i, block, along):
            dims = (rows, 1) if along == 0 else (1, rows)
            at = lax.broadcasted_iota(jnp.int32, dims, along)
            pos = at + i[ORDER + block * slots] * blk
            for s in range(1, slots):
                moved = at - s * blk + i[ORDER + block * slots + s] * blk
                pos = jnp.where(at >= s * blk, moved, pos)
            return pos

        def fill_positions(i, kpos, qpos):
            for e in range(n_ctx):
                here = slice(e * rows, (e + 1) * rows)
                kpos[:, here] = positions(i, i[CI] ^ e, 1)
                qpos[here, :] = positions(i, i[CI] ^ e, 0)

        tall = 2 * rows
        places = [pltpu.VMEM((1, length), jnp.int32), pltpu.VMEM((length, 1), jnp.int32)]

        def attend(i, *refs):
            got, refs = refs[:n_ctx], refs[n_ctx:]
            seq, att, lse_ref, refs = refs[0], refs[1], refs[2], refs[3:]
            send, (kpos, qpos) = refs[:n_f], refs[n_f:]
            for e in range(n_ctx):
                seq[e * rows : (e + 1) * rows, :] = got[e][...]
            fill_positions(i, kpos, qpos)

            def step(e, _):
                here = pl.ds(pl.multiple_of(e * tall, tall), tall)
                allowed = kpos[...] <= qpos[here, :]
                for h in range(heads):
                    cut = slice(h * hd, (h + 1) * hd)
                    keys = seq[:, pair + h * hd : pair + (h + 1) * hd]
                    values = seq[:, 2 * pair + h * hd : 2 * pair + (h + 1) * hd]
                    scores = jnp.where(allowed, through(seq[here, cut], keys), -1e30)
                    top = jnp.max(scores, axis=1, keepdims=True)
                    probs = jnp.exp(scores - top)
                    norm = jnp.sum(probs, axis=1, keepdims=True)
                    out = dot(probs.astype(BF), values) / norm
                    att[here, cut] = out.astype(BF)
                    lse_ref[here, cut] = jnp.broadcast_to(top + jnp.log(norm), (tall, hd))
                return 0

            lax.fori_loop(0, length // tall, step, 0)
            for m in range(n_f):
                for core in range(2):
                    block = (2 * (m ^ i[FI]) + core) ^ i[CI]
                    at = pl.multiple_of(block * rows, rows)
                    send[m][core * rows : (core + 1) * rows, :] = att[pl.ds(at, rows), :]

        outs = [shaped((length, 3 * pair), BF), shaped((length, pair), BF), shaped((length, pair), F32)]
        outs += [shaped((tall, pair), BF)] * n_f
        seq, att, lse, *sends = call(
            attend, outs, idx, got, places, flops=4 * length * length * pair
        )
        got = [both_to(sends[m], lambda i, f: (2 * (m ^ f) + i % 2, i // 2)) for m in range(n_f)]
        o_parts = got + [ctx_to(g, 1) for g in got]

        def o_part(i, refs, core, m):
            here = pl.ds(pl.multiple_of(i[CORE] * rows, rows), rows)
            own, other = refs[m][here, :], refs[n_f + m][here, :]
            return jnp.where(core == i[CORE], own, other)

        def finish(i, *refs):
            x_ref, small_ref, refs = refs[0], refs[1], refs[2:]
            o_refs, refs = refs[: 2 * n_f], refs[2 * n_f :]
            own, refs = refs[0], refs[1:]
            got_o, refs = refs[: n_f - 1], refs[n_f - 1 :]
            other_o, refs = refs[: n_f - 1], refs[n_f - 1 :]
            mid_ref, a_ref, full = refs
            fill_rows(full, own, got_o, other_o, i[FI], i[CORE], slice(hidden, None))
            mid = x_ref[...] + small_ref[5:6, :]
            for m in range(n_f):
                for core in range(2):
                    at = pl.multiple_of((2 * (m ^ i[Z]) + core) * pair, pair)
                    mid = mid + dot(o_part(i, o_refs, core, m), full[pl.ds(at, pair), :])
            mid_ref[...] = mid
            normed, _ = normalize(mid)
            a_ref[...] = (normed * small_ref[1:2, :] + small_ref[6:7, :]).astype(BF)

        outs = [shaped((rows, width), F32), shaped((rows, width), BF), shaped((width, width), BF)]
        mid, a_two, full_out = call(
            finish, outs, idx,
            [x, small] + o_parts + [own_w] + got_w + other_w,
            flops=2 * rows * width * width,
        )
        a2_parts = gather_f(a_two)

        def forward(i, *refs):
            a_refs, refs = refs[:n_f], refs[n_f:]
            own_w_ref, bias, refs = refs[0], refs[1], refs[2:]
            got_u, other_u = refs[: n_f - 1], refs[n_f - 1 : 2 * n_f - 2]
            up, a_ref, gel, slope_ref = refs[2 * n_f - 2 :]
            fill_rows(up, own_w_ref, got_u, other_u, i[FI], i[CORE], slice(0, hidden))
            for k in range(n_f):
                here = pl.ds(pl.multiple_of((i[FI] ^ k) * rows, rows), rows)
                a_two = a_refs[k][...]
                a_ref[here, :] = a_two
                value, slope = gelu_parts(dot(a_two, up[...]) + bias[...].astype(F32))
                gel[here, :] = value.astype(BF)
                slope_ref[here, :] = slope.astype(BF)

        outs = [
            shaped((width, hidden), BF),
            shaped((all_rows, width), BF),
            shaped((all_rows, hidden), BF),
            shaped((all_rows, hidden), BF),
        ]
        full_up, a2_all, gelled, slope = call(
            forward, outs, idx, a2_parts + [own_w, up_bias] + got_w + other_w,
            flops=2 * all_rows * width * hidden,
        )
        g_down = outer(gelled, dz_all).astype(BF)

        def scatter_ctx(g):
            return lax.psum_scatter(g, "ctx", scatter_dimension=0, tiled=True)

        part_down = scatter_ctx(g_down)

        def backward(i, dz_ref, slope_ref, down, up, du_ref, sum_ref, own, *send):
            total = jnp.zeros((1, hidden), F32)
            for k in range(n_f):
                here = pl.ds(pl.multiple_of((i[FI] ^ k) * rows, rows), rows)
                d_pre = through(dz_ref[here, :], down[...]) * slope_ref[here, :].astype(F32)
                total = total + jnp.sum(d_pre, axis=0, keepdims=True)
                d_hidden = d_pre.astype(BF)
                du_ref[here, :] = d_hidden
                part = through(d_hidden, up[...])
                if k:
                    send[k - 1][...] = part.astype(BF)
                else:
                    own[...] = part
            sum_ref[...] = total

        outs = [
            shaped((all_rows, hidden), BF),
            shaped((1, hidden), F32),
            shaped((rows, width), F32),
        ] + [shaped((rows, width), BF)] * (n_f - 1)
        d_hidden, up_sum, d_own, *sends = call(
            backward, outs, idx, [dz_all, slope, w_down, full_up],
            flops=4 * all_rows * width * hidden, mib=54,
        )
        got_a = send_f(sends)
        g_up = outer(a2_all, d_hidden).astype(BF)

        part_up = scatter_ctx(g_up)

        def second(i, *refs):
            d_ref, mid_ref, small_ref, full, own, refs = (*refs[:5], refs[5:])
            got, refs = refs[: n_f - 1], refs[n_f - 1 :]
            dmid_ref, dy_ref, sums, send = refs[0], refs[1], refs[2], refs[3:]
            d_a = own[...]
            for g in got:
                d_a = d_a + g[...].astype(F32)
            normed, inv = normalize(mid_ref[...])
            d_res = d_ref[...]
            d_mid = d_res + norm_back(d_a * small_ref[1:2, :], normed, inv)
            dmid_ref[...] = d_mid
            dy = d_mid.astype(BF)
            dy_ref[...] = dy
            for m in range(n_f):
                at = pl.multiple_of((m ^ i[Z]) * wide, wide)
                send[m][...] = through(dy, full[pl.ds(at, wide), :]).astype(BF)
            sums[...] = jnp.zeros_like(sums)
            sums[1:2, :] = jnp.sum(d_a * normed, axis=0, keepdims=True)
            sums[5:6, :] = jnp.sum(d_mid, axis=0, keepdims=True)
            sums[6:7, :] = jnp.sum(d_a, axis=0, keepdims=True)
            sums[7:8, :] = jnp.sum(d_res, axis=0, keepdims=True)

        outs = [shaped((rows, width), F32), shaped((rows, width), BF), shaped((8, width), F32)]
        outs += [shaped((rows, wide), BF)] * n_f
        d_mid, dy, sums, *sends = call(
            second, outs, idx, [d_result, mid, small, full_out, d_own] + got_a,
            flops=2 * rows * width * width,
        )
        got = [both_to(sends[m], lambda i, f: (2 * f + i % 2, m ^ (i // 2))) for m in range(n_f)]
        got += [ctx_to(g, 1) for g in got]

        def attend_back(i, *refs):
            seq_ref, att_ref, lse_ref, refs = refs[0], refs[1], refs[2], refs[3:]
            got, refs = refs[: 2 * n_f], refs[2 * n_f :]
            sum_ref, refs = refs[0], refs[1:]
            send, (kpos, qpos, d_out, d_query, d_keys, d_values) = refs[:n_ctx], refs[n_ctx:]
            fill_positions(i, kpos, qpos)
            for m in range(n_f):
                for swap in range(2):
                    part = got[swap * n_f + m]
                    block = (2 * (m ^ i[FI]) + (i[CORE] ^ swap)) ^ i[CI]
                    at = pl.multiple_of(block * rows, rows)
                    d_out[pl.ds(at, rows), :] = jnp.where(
                        i[CORE] == 0, part[:, :pair], part[:, pair:]
                    )
            d_keys[...] = jnp.zeros_like(d_keys)
            d_values[...] = jnp.zeros_like(d_values)

            def step(e, _):
                here = pl.ds(pl.multiple_of(e * tall, tall), tall)
                allowed = kpos[...] <= qpos[here, :]
                for h in range(heads):
                    cut = slice(h * hd, (h + 1) * hd)
                    query, d_att = seq_ref[here, cut], d_out[here, cut]
                    keys = seq_ref[:, pair + h * hd : pair + (h + 1) * hd]
                    values = seq_ref[:, 2 * pair + h * hd : 2 * pair + (h + 1) * hd]
                    lse = lse_ref[here, h * hd : h * hd + 1]
                    scores = jnp.where(allowed, through(query, keys), -1e30)
                    probs = jnp.exp(scores - lse)
                    delta = jnp.sum(
                        d_att.astype(F32) * att_ref[here, cut].astype(F32), axis=1, keepdims=True
                    )
                    d_scores = (probs * (through(d_att, values) - delta)).astype(BF)
                    d_query[here, cut] = dot(d_scores, keys) * SCALE
                    d_keys[:, cut] += outer(d_scores, query)
                    d_values[:, cut] += outer(probs.astype(BF), d_att)
                return 0

            lax.fori_loop(0, length // tall, step, 0)
            for e in range(n_ctx):
                here = slice(e * rows, (e + 1) * rows)
                send[e][:, :pair] = d_query[here, :].astype(BF)
                send[e][:, pair : 2 * pair] = d_keys[here, :].astype(BF)
                send[e][:, 2 * pair :] = d_values[here, :].astype(BF)
            sum_ref[...] = jnp.zeros_like(sum_ref)
            sum_ref[3:4, :] = jnp.sum(d_query[...], axis=0, keepdims=True)
            sum_ref[4:5, :] = jnp.sum(d_values[...], axis=0, keepdims=True)

        outs = [shaped((8, pair), F32)] + [shaped((rows, 3 * pair), BF)] * n_ctx
        qv_sum, *sends = call(
            attend_back, outs, idx, [seq, att, lse] + got,
            places
            + [
                pltpu.VMEM((length, pair), BF),
                pltpu.VMEM((length, pair), F32),
                pltpu.VMEM((length, pair), F32),
                pltpu.VMEM((length, pair), F32),
            ],
            flops=10 * length * length * pair,
        )
        got = [sends[0]] + [ctx_to(sends[e], e) for e in range(1, n_ctx)]

        n_all_dev = n_ctx * n_f
        per = width // n_all_dev

        def grad_out(i, dy_ref, *refs):
            o_refs, (away, keep, held) = refs[: 2 * n_f], refs[2 * n_f :]
            for m in range(n_f):
                for core in range(2):
                    at = pl.multiple_of((2 * (m ^ i[Z]) + core) * pair, pair)
                    held[pl.ds(at, pair), :] = outer(o_part(i, o_refs, core, m), dy_ref[...])
            for b in range(n_z):
                for f in range(n_f):
                    at = (2 * b + i[CORE]) * n_f * per + f * per
                    keep[f, b * per : (b + 1) * per, :] = held[pl.ds(at, per), :]
                    at = (2 * b + 1 - i[CORE]) * n_f * per + f * per
                    away[f, b * per : (b + 1) * per, :] = held[pl.ds(at, per), :].astype(BF)

        dims = (n_f, n_z * per, width)
        away, out_keep = call(
            grad_out, [shaped(dims, BF), shaped(dims, F32)], idx, [dy] + o_parts,
            [pltpu.VMEM((width, width), F32)], flops=2 * rows * width * width,
        )
        away = ctx_to(away, 1)

        def out_first(i, keep, got, own, *send):
            f = i[FI]
            own[...] = keep[f] + got[f].astype(F32)
            for k in range(1, n_f):
                send[k - 1][...] = (keep[f ^ k] + got[f ^ k].astype(F32)).astype(BF)

        outs = [shaped((n_z * per, width), F32)] + [shaped((n_z * per, width), BF)] * (n_f - 1)
        out_own, *sends = call(out_first, outs, idx, [out_keep, away])
        out_got = send_f(sends)

        def out_second(i, own_ref, *refs):
            got, (own, *send), held = refs[: n_f - 1], refs[n_f - 1 : -1], refs[-1]
            total = own_ref[...]
            for g in got:
                total = total + g[...].astype(F32)
            held[...] = total
            own[...] = held[pl.ds(pl.multiple_of(i[Z] * per, per), per), :]
            for m in range(1, n_z):
                at = pl.ds(pl.multiple_of((i[Z] ^ m) * per, per), per)
                send[m - 1][...] = held[at, :].astype(BF)

        outs = [shaped((per, width), F32)] + [shaped((per, width), BF)] * (n_z - 1)
        out_own, *sends = call(
            out_second, outs, idx, [out_own] + out_got,
            [pltpu.VMEM((n_z * per, width), F32)],
        )
        out_got = [ctx_to(s, 2 * (m + 1)) for m, s in enumerate(sends)]

        def first(i, *refs):
            got, refs = refs[:n_ctx], refs[n_ctx:]
            n_refs, refs = refs[:n_f], refs[n_f:]
            full, sum_in, refs = refs[0], refs[1], refs[2:]
            proj_ref, sums, own, send, held = refs[0], refs[1], refs[2], refs[3:-1], refs[-1]
            for e in range(n_ctx):
                held[e] = got[e][...]
            gain_sum = jnp.zeros((1, width), F32)
            shift_sum = jnp.zeros((1, width), F32)
            for k in range(n_f):
                here = slice(k * rows, (k + 1) * rows)
                for p in range(2):
                    e = 2 * (i[FI] ^ i[Z] ^ k) + (i[CORE] ^ p)
                    for q in range(3):
                        at = q * wide + p * pair
                        proj_ref[here, at : at + pair] = held[e, :, q * pair : (q + 1) * pair]
                part = through(proj_ref[here, :], full[...])
                gain_sum += jnp.sum(part * n_refs[k][...].astype(F32), axis=0, keepdims=True)
                shift_sum += jnp.sum(part, axis=0, keepdims=True)
                if k:
                    send[k - 1][...] = part.astype(BF)
                else:
                    own[...] = part
            sums[...] = sum_in[...]
            sums[0:1, :] = gain_sum
            sums[2:3, :] = shift_sum

        outs = [
            shaped((all_rows, 3 * wide), BF),
            shaped((8, width), F32),
            shaped((rows, width), F32),
        ] + [shaped((rows, width), BF)] * (n_f - 1)
        d_proj, sums, d_own, *sends = call(
            first, outs, idx, got + n_all + [full_qkv, sums],
            [pltpu.VMEM((n_ctx, rows, 3 * pair), BF)],
            flops=6 * all_rows * width * wide, mib=54,
        )
        got_x = send_f(sends)

        block = width // n_ctx
        per_up = hidden // n_ctx

        def pack(i, a_ref, p_ref, sums_ref, up_ref, qv_ref, away, keep, held):
            f, core = i[FI], i[CORE]
            for zz in range(n_z):
                at = slice(2 * zz * block, 2 * (zz + 1) * block)
                held[...] = outer(a_ref[:, at], p_ref[...])
                both = sums_ref[:, at]
                for par, out in ((core, keep), (1 - core, away)):
                    row = pl.ds(pl.multiple_of(par * block, block), block)
                    out[zz, :block, :] = held[row, :].astype(out.dtype)
                    out[zz, block:, :] = jnp.zeros((16, 3 * wide), out.dtype)
                    hit = jnp.logical_and(zz == f, par == core)
                    small = jnp.where(par == 0, both[:, :block], both[:, block:])
                    small = small + jnp.where(hit, qv_ref[...], 0.0)
                    ups = up_ref[:, pl.ds(pl.multiple_of(par * n_f * per_up, n_f * per_up), n_f * per_up)]
                    ups = jnp.where(zz == f, ups, 0.0)
                    out[zz, block : block + 8, :block] = small.astype(out.dtype)
                    for g in range(n_f):
                        out[zz, block + 8 + g : block + 9 + g, :per_up] = ups[
                            :, g * per_up : (g + 1) * per_up
                        ].astype(out.dtype)

        dims = (n_z, block + 16, 3 * wide)
        away, keep = call(
            pack, [shaped(dims, BF), shaped(dims, F32)], idx,
            [a_all, d_proj, sums, up_sum, qv_sum], [pltpu.VMEM((2 * block, 3 * wide), F32)],
            flops=6 * all_rows * width * wide,
        )
        away = ctx_to(away, 1)

        def over_core(i, keep_ref, got, own, *send):
            own[...] = keep_ref[i[Z]] + got[i[Z]].astype(F32)
            for m in range(1, n_z):
                at = i[Z] ^ m
                send[m - 1][...] = (keep_ref[at] + got[at].astype(F32)).astype(BF)

        outs = [shaped(dims[1:], F32)] + [shaped(dims[1:], BF)] * (n_z - 1)
        own, *sends = call(over_core, outs, idx, [keep, away])
        got = [ctx_to(s, 2 * (m + 1)) for m, s in enumerate(sends)]
        low_down = both_to(part_down, lambda i, f: ((f * n_ctx + i) // n_f, (f * n_ctx + i) % n_f))

        def down(i, gel, w_ref, own, *send):
            for k in range(n_f):
                here = pl.ds(pl.multiple_of((i[FI] ^ k) * rows, rows), rows)
                part = dot(gel[here, :], w_ref[...])
                if k:
                    send[k - 1][...] = part.astype(BF)
                else:
                    own[...] = part

        outs = [shaped((rows, width), F32)] + [shaped((rows, width), BF)] * (n_f - 1)
        z_own, *sends = call(down, outs, idx, [gelled, w_down], flops=2 * all_rows * width * hidden)
        z_got = send_f(sends)

        def add_up(i, own, mid_ref, small_ref, o_ref, *refs):
            got, got_o, (out, o_sum) = refs[: n_f - 1], refs[n_f - 1 : -2], refs[-2:]
            total = own[...]
            for g in got:
                total = total + g[...].astype(F32)
            out[...] = total + mid_ref[...] + small_ref[7:8, :]
            total = o_ref[...]
            for g in got_o:
                total = total + g[...].astype(F32)
            o_sum[...] = total

        result, out_out = call(
            add_up, [shaped((rows, width), F32), shaped((per, width), F32)], idx,
            [z_own, mid, small, out_own] + z_got + out_got,
        )

        def input_grad(i, x_ref, dmid_ref, small_ref, low_ref, own, *refs):
            got, (out, wider) = refs[:-2], refs[-2:]
            normed, inv = normalize(x_ref[...])
            d_a = own[...]
            for g in got:
                d_a = d_a + g[...].astype(F32)
            out[...] = dmid_ref[...] + norm_back(d_a * small_ref[0:1, :], normed, inv)
            wider[...] = low_ref[...].astype(F32)

        outs = [shaped((rows, width), F32), shaped(low_down.shape, F32)]
        d_input, out_down = call(input_grad, outs, idx, [x, d_mid, small, low_down, d_own] + got_x)

        def over_z(i, *refs):
            own_ref, got, up_ref, refs = refs[0], refs[1:n_z], refs[n_z], refs[n_z + 1 :]
            own, send, (held, held_up) = refs[0], refs[1:-2], refs[-2:]
            total = own_ref[...]
            for g in got:
                total = total + g[...].astype(F32)
            held[...] = total
            held_up[...] = up_ref[...].astype(F32)
            for k in range(n_f):
                at = pl.ds(pl.multiple_of((i[FI] ^ k) * per, per), per)
                out = send[k - 1] if k else own
                out[:per, : 3 * wide] = held[at, : 3 * wide].astype(out.dtype)
                out[:per, 3 * wide :] = held_up[at, :].astype(out.dtype)
                out[per:, :] = jnp.zeros((16, 3 * wide + hidden), out.dtype)
                out[per:, : 3 * wide] = held[block:, : 3 * wide].astype(out.dtype)

        dims = (per + 16, 3 * wide + hidden)
        outs = [shaped(dims, F32)] + [shaped(dims, BF)] * (n_f - 1)
        own, *sends = call(
            over_z, outs, idx, [own] + got + [part_up],
            [pltpu.VMEM((block + 16, 3 * wide), F32), pltpu.VMEM((block, hidden), F32)],
            mib=54,
        )
        got = send_f(sends)

        def last(i, own_ref, *refs):
            got, (out, up, small_ref, bias_ref) = refs[: n_f - 1], refs[n_f - 1 :]
            total = own_ref[per:, :block]
            for k in range(n_f):
                src = got[k - 1] if k else own_ref
                for q in range(3):
                    at = pl.ds(pl.multiple_of(q * width + (i[FI] ^ k) * wide, wide), wide)
                    out[:, at] = src[:per, q * wide : (q + 1) * wide].astype(F32)
                at = pl.ds(pl.multiple_of((i[FI] ^ k) * hidden, hidden), hidden)
                up[:, at] = src[:per, 3 * wide :].astype(F32)
                if k:
                    total = total + src[per:, :block].astype(F32)
            share, ups = total[:8, :per], total[8:9, :per_up]
            for g in range(1, n_f):
                share = jnp.where(i[FI] == g, total[:8, g * per : (g + 1) * per], share)
                ups = jnp.where(i[FI] == g, total[8 + g : 9 + g, :per_up], ups)
            small_ref[...] = share
            bias_ref[...] = ups

        outs = [shaped((per, 3 * width), F32), shaped((per, n_f * hidden), F32)]
        outs += [shaped((8, per), F32), shaped((1, per_up), F32)]
        out_qkv, out_up, out_small, out_upb = call(last, outs, idx, [own] + got)

        shape = (seqs, slots, blk, width)
        return (
            result.reshape(shape),
            d_input.reshape(shape),
            out_qkv[None],
            out_out[None],
            out_up[None],
            out_down[None],
            out_small[:2][None],
            out_small[2:][None],
            out_upb.reshape(1, -1),
        )

    return layer


def solution(mesh):
    return jax.shard_map(
        build(mesh),
        mesh=mesh,
        in_specs=(
            P("fsdp", "ctx", None, None),
            P(),
            P(None, "fsdp", None),
            P(None, "fsdp", None),
            P(None, "fsdp", None),
            P(None, "fsdp", None),
            P(None, None, "fsdp"),
            P(None, None, "fsdp"),
            P(None, "fsdp"),
            P("fsdp", "ctx", None, None),
        ),
        out_specs=(
            P("fsdp", "ctx", None, None),
            P("fsdp", "ctx", None, None),
            P(None, ("ctx", "fsdp"), None),
            P(None, ("ctx", "fsdp"), None),
            P(None, ("ctx", "fsdp"), None),
            P(None, ("ctx", "fsdp"), None),
            P(None, None, ("ctx", "fsdp")),
            P(None, None, ("ctx", "fsdp")),
            P(None, ("ctx", "fsdp")),
        ),
        check_vma=False,
    )
```

```python
import functools

import jax
import jax.numpy as jnp
from jax import lax
from jax.experimental import pallas as pl
from jax.experimental.pallas import tpu as pltpu
from jax.sharding import PartitionSpec as P


HEADS = 16
EPS = 1e-05
SCALE = 0.125
GELU_C = 0.7978845608028654
BF = jnp.bfloat16
F32 = jnp.float32


CI, FI, Z, CORE, ORDER = 0, 1, 2, 3, 8


def normalize(x):
    centred = x - jnp.mean(x, axis=1, keepdims=True)
    inv = lax.rsqrt(jnp.mean(centred * centred, axis=1, keepdims=True) + EPS)
    return (centred * inv, inv)


def norm_back(grad, normed, inv):
    return inv * (
        grad
        - jnp.mean(grad, axis=1, keepdims=True)
        - normed * jnp.mean(grad * normed, axis=1, keepdims=True)
    )


def gelu_parts(u):
    inner = GELU_C * (u + 0.044715 * u * u * u)
    tanhed = jnp.tanh(inner)
    value = 0.5 * u * (1.0 + tanhed)
    slope = 0.5 * (1.0 + tanhed) + 0.5 * u * (1.0 - tanhed * tanhed) * GELU_C * (
        1.0 + 3.0 * 0.044715 * u * u
    )
    return (value, slope)


def dot(a, b):
    return jnp.dot(a, b, preferred_element_type=F32)


def outer(left, right):
    return lax.dot_general(left, right, (((0,), (0,)), ((), ())), preferred_element_type=F32)


def through(left, weight):
    return lax.dot_general(left, weight, (((1,), (1,)), ((), ())), preferred_element_type=F32)


def shaped(shape, kind):
    return jax.ShapeDtypeStruct(shape, kind)


def total_bytes(arrays):
    return sum(a.size * a.dtype.itemsize for a in arrays)


def call(kernel, outs, idx, ins, scratch=(), flops=0, mib=20):
    vmem = pl.BlockSpec(memory_space=pltpu.VMEM)
    return pl.pallas_call(
        kernel,
        out_shape=outs,
        in_specs=[pl.BlockSpec(memory_space=pltpu.SMEM)] + [vmem] * len(ins),
        out_specs=[vmem] * len(outs),
        scratch_shapes=list(scratch),
        compiler_params=pltpu.CompilerParams(vmem_limit_bytes=mib * 1024 * 1024),
        cost_estimate=pl.CostEstimate(
            flops=flops, bytes_accessed=total_bytes(ins) + total_bytes(outs), transcendentals=0
        ),
    )(idx, *ins)


def build(mesh):
    n_ctx, n_f = mesh.shape["ctx"], mesh.shape["fsdp"]
    n_z = n_ctx // 2

    def fsdp_to(x, k):
        return lax.ppermute(x, "fsdp", [(f, f ^ k) for f in range(n_f)])

    def ctx_to(x, e):
        return lax.ppermute(x, "ctx", [(i, i ^ e) for i in range(n_ctx)])

    def both_to(x, target):
        pairs = []
        for i in range(n_ctx):
            for f in range(n_f):
                to_i, to_f = target(i, f)
                pairs.append((i * n_f + f, to_i * n_f + to_f))
        return lax.ppermute(x, ("ctx", "fsdp"), pairs)

    def gather_f(block):
        return [block] + [fsdp_to(block, k) for k in range(1, n_f)]

    def send_f(blocks):
        return [fsdp_to(b, k + 1) for k, b in enumerate(blocks)]

    def share_core(blocks):
        return [ctx_to(b, 1) for b in blocks]

    def fill_rows(full, own, got, other, fi, core, cut=slice(None)):
        depth = own.shape[0]
        half = depth // 2
        full[pl.ds(fi * depth, depth), :] = own[:, cut]
        for k in range(1, n_f):
            base = (fi ^ k) * depth
            full[pl.ds(base + core * half, half), :] = got[k - 1][:half, cut]
            full[pl.ds(base + (1 - core) * half, half), :] = other[k - 1][:half, cut]

    def layer(inputs, block_order, w_qkv, w_out, w_up, w_down, gains, biases, up_bias, out_grad):
        seqs, slots, blk, width = inputs.shape
        rows = seqs * slots * blk
        ci = lax.axis_index("ctx")
        fi = lax.axis_index("fsdp")
        z, c = ci // 2, ci % 2
        mine = 2 * fi + c
        wide = width // n_f
        pair = wide // 2
        hidden = up_bias.shape[1]
        hd = width // HEADS
        heads = pair // hd
        length = n_ctx * rows
        half = wide // 2
        all_rows = n_f * rows
        x = inputs.reshape(rows, width)
        d_result = out_grad.reshape(rows, width)
        w_qkv, w_out, w_up, w_down = w_qkv[0], w_out[0], w_up[0], w_down[0]
        zero = jnp.zeros((), jnp.int32)
        idx = jnp.concatenate(
            [jnp.stack([ci, fi, z, c, mine, zero, zero, zero]).astype(jnp.int32), block_order]
        )
        own_small = jnp.concatenate([gains[0], biases[0]])
        n_small = own_small.shape[0]

        def prep(i, x_ref, w_ref, s_ref, n_ref, own_ref, *send):
            normed, _ = normalize(x_ref[...])
            n_ref[...] = normed.astype(BF)
            f, core = i[FI], i[CORE]
            for q in range(3):
                to = slice(q * wide, (q + 1) * wide)
                at = pl.multiple_of(q * width + f * wide, wide)
                own_ref[:, to] = w_ref[:, pl.ds(at, wide)]
                for k in range(1, n_f):
                    at = pl.multiple_of(q * width + (f ^ k) * wide, wide)
                    row = pl.multiple_of(core * half, half)
                    send[k - 1][:half, to] = w_ref[pl.ds(row, half), pl.ds(at, wide)]
            for k in range(1, n_f):
                send[k - 1][half : half + n_small, :wide] = s_ref[...]

        outs = [shaped((rows, width), BF), shaped((wide, 3 * wide), BF)]
        outs += [shaped((half + 16, 3 * wide), BF)] * (n_f - 1)
        n_one, own_qkv, *sends = call(prep, outs, idx, [x, w_qkv, own_small])
        got_qkv = send_f(sends)
        other_qkv = share_core(got_qkv)
        n_all = gather_f(n_one)

        def project(i, *refs):
            n_refs, refs = refs[:n_f], refs[n_f:]
            own, s_ref, refs = refs[0], refs[1], refs[2:]
            got, refs = refs[: n_f - 1], refs[n_f - 1 :]
            other, refs = refs[: n_f - 1], refs[n_f - 1 :]
            a_ref, full, small, refs = refs[0], refs[1], refs[2], refs[3:]
            send, held = refs[:n_ctx], refs[n_ctx]
            f, core = i[FI], i[CORE]
            for k in range(n_f):
                piece = s_ref[...] if k == 0 else got[k - 1][half : half + n_small, :wide]
                small[:, pl.ds(pl.multiple_of((f ^ k) * wide, wide), wide)] = piece.astype(F32)
            fill_rows(full, own, got, other, f, core)
            at = pl.ds(pl.multiple_of(f * wide, wide), wide)
            q_shift, v_shift = small[3:4, at], small[4:5, at]
            for k in range(n_f):
                a_one = (n_refs[k][...].astype(F32) * small[0:1, :] + small[2:3, :]).astype(BF)
                a_ref[k * rows : (k + 1) * rows, :] = a_one
                proj = dot(a_one, full[...])
                query = ((proj[:, :wide] + q_shift) * SCALE).astype(BF)
                keys = proj[:, wide : 2 * wide].astype(BF)
                values = (proj[:, 2 * wide :] + v_shift).astype(BF)
                for p in range(2):
                    cut = slice(p * pair, (p + 1) * pair)
                    for q, part in enumerate((query, keys, values)):
                        held[k, p, :, q * pair : (q + 1) * pair] = part[:, cut]
            for e in range(n_ctx):
                send[e][...] = held[i[FI] ^ i[Z] ^ (e >> 1), core ^ (e & 1)]

        outs = [
            shaped((all_rows, width), BF),
            shaped((width, 3 * wide), BF),
            shaped((n_small, width), F32),
        ] + [shaped((rows, 3 * pair), BF)] * n_ctx
        a_all, full_qkv, small, *sends = call(
            project, outs, idx,
            n_all + [own_qkv, own_small] + got_qkv + other_qkv,
            [pltpu.VMEM((n_f, 2, rows, 3 * pair), BF)],
            flops=6 * all_rows * width * wide,
        )
        got = [sends[0]] + [ctx_to(sends[e], e) for e in range(1, n_ctx)]

        def cut_weights(i, up_ref, out_ref, own_ref, *send):
            f, core = i[FI], i[CORE]
            row = pl.ds(pl.multiple_of(core * half, half), half)
            own_ref[:, :hidden] = up_ref[:, pl.ds(pl.multiple_of(f * hidden, hidden), hidden)]
            own_ref[:, hidden:] = out_ref[...]
            for k in range(1, n_f):
                at = pl.ds(pl.multiple_of((f ^ k) * hidden, hidden), hidden)
                send[k - 1][:, :hidden] = up_ref[row, at]
                send[k - 1][:, hidden:] = out_ref[row, :]

        outs = [shaped((wide, hidden + width), BF)]
        outs += [shaped((half, hidden + width), BF)] * (n_f - 1)
        own_w, *sends = call(cut_weights, outs, idx, [w_up, w_out])
        got_w = send_f(sends)
        other_w = share_core(got_w)
        dz, _ = lax.optimization_barrier((d_result.astype(BF), n_all))
        dz_all = lax.all_gather(dz, "fsdp", axis=0, tiled=True)

        low_rows = length // 2

        def place(i, block, slot):
            late = i[ORDER + (i[CI] ^ block) * slots + slot] >= n_ctx * slots // 2
            return pl.multiple_of(jnp.where(late, low_rows, 0) + block * blk, blk)

        def fill_positions(i, kpos, qpos):
            along = lax.broadcasted_iota(jnp.int32, (1, blk), 1)
            down_to = lax.broadcasted_iota(jnp.int32, (blk, 1), 0)
            for e in range(n_ctx):
                at = ORDER + (i[CI] ^ e) * slots
                early = jnp.minimum(i[at], i[at + 1]) * blk
                late = jnp.maximum(i[at], i[at + 1]) * blk
                for base, start in ((0, early), (low_rows, late)):
                    here = slice(base + e * blk, base + (e + 1) * blk)
                    kpos[:, here] = start + along
                    qpos[here, :] = start + down_to

        tall = 2 * rows
        places = [pltpu.VMEM((1, length), jnp.int32), pltpu.VMEM((length, 1), jnp.int32)]

        def attend(i, *refs):
            got, refs = refs[:n_ctx], refs[n_ctx:]
            seq, att, lse_ref, refs = refs[0], refs[1], refs[2], refs[3:]
            send, (kpos, qpos) = refs[:n_f], refs[n_f:]
            for e in range(n_ctx):
                for j in range(slots):
                    seq[pl.ds(place(i, e, j), blk), :] = got[e][j * blk : (j + 1) * blk, :]
            fill_positions(i, kpos, qpos)

            def step(span, e, _):
                here = pl.ds(pl.multiple_of(e * tall, tall), tall)
                allowed = kpos[:, :span] <= qpos[here, :]
                for h in range(heads):
                    cut = slice(h * hd, (h + 1) * hd)
                    keys = seq[:span, pair + h * hd : pair + (h + 1) * hd]
                    values = seq[:span, 2 * pair + h * hd : 2 * pair + (h + 1) * hd]
                    scores = jnp.where(allowed, through(seq[here, cut], keys), -1e30)
                    top = jnp.max(scores, axis=1, keepdims=True)
                    probs = jnp.exp(scores - top)
                    norm = jnp.sum(probs, axis=1, keepdims=True)
                    out = dot(probs.astype(BF), values) / norm
                    att[here, cut] = out.astype(BF)
                    lse_ref[here, cut] = jnp.broadcast_to(top + jnp.log(norm), (tall, hd))
                return 0

            steps = low_rows // tall
            lax.fori_loop(0, steps, functools.partial(step, low_rows), 0)
            lax.fori_loop(steps, 2 * steps, functools.partial(step, length), 0)
            for m in range(n_f):
                for core in range(2):
                    block = (2 * (m ^ i[FI]) + core) ^ i[CI]
                    for j in range(slots):
                        to = core * rows + j * blk
                        send[m][to : to + blk, :] = att[pl.ds(place(i, block, j), blk), :]

        outs = [shaped((length, 3 * pair), BF), shaped((length, pair), BF), shaped((length, pair), F32)]
        outs += [shaped((tall, pair), BF)] * n_f
        seq, att, lse, *sends = call(
            attend, outs, idx, got, places, flops=4 * length * length * pair
        )
        got = [both_to(sends[m], lambda i, f: (2 * (m ^ f) + i % 2, i // 2)) for m in range(n_f)]
        o_parts = got + [ctx_to(g, 1) for g in got]

        def o_part(i, refs, core, m):
            here = pl.ds(pl.multiple_of(i[CORE] * rows, rows), rows)
            own, other = refs[m][here, :], refs[n_f + m][here, :]
            return jnp.where(core == i[CORE], own, other)

        def finish(i, *refs):
            x_ref, small_ref, refs = refs[0], refs[1], refs[2:]
            o_refs, refs = refs[: 2 * n_f], refs[2 * n_f :]
            own, refs = refs[0], refs[1:]
            got_o, refs = refs[: n_f - 1], refs[n_f - 1 :]
            other_o, refs = refs[: n_f - 1], refs[n_f - 1 :]
            mid_ref, a_ref, full = refs
            fill_rows(full, own, got_o, other_o, i[FI], i[CORE], slice(hidden, None))
            mid = x_ref[...] + small_ref[5:6, :]
            for m in range(n_f):
                for core in range(2):
                    at = pl.multiple_of((2 * (m ^ i[Z]) + core) * pair, pair)
                    mid = mid + dot(o_part(i, o_refs, core, m), full[pl.ds(at, pair), :])
            mid_ref[...] = mid
            normed, _ = normalize(mid)
            a_ref[...] = (normed * small_ref[1:2, :] + small_ref[6:7, :]).astype(BF)

        outs = [shaped((rows, width), F32), shaped((rows, width), BF), shaped((width, width), BF)]
        mid, a_two, full_out = call(
            finish, outs, idx,
            [x, small] + o_parts + [own_w] + got_w + other_w,
            flops=2 * rows * width * width,
        )
        a2_parts = gather_f(a_two)

        def forward(i, *refs):
            a_refs, refs = refs[:n_f], refs[n_f:]
            own_w_ref, bias, refs = refs[0], refs[1], refs[2:]
            got_u, other_u = refs[: n_f - 1], refs[n_f - 1 : 2 * n_f - 2]
            dz_ref, up, a_ref, gel, slope_ref, g_ref = refs[2 * n_f - 2 :]
            fill_rows(up, own_w_ref, got_u, other_u, i[FI], i[CORE], slice(0, hidden))
            for k in range(n_f):
                here = pl.ds(pl.multiple_of((i[FI] ^ k) * rows, rows), rows)
                a_two = a_refs[k][...]
                a_ref[here, :] = a_two
                value, slope = gelu_parts(dot(a_two, up[...]) + bias[...].astype(F32))
                gel[here, :] = value.astype(BF)
                slope_ref[here, :] = slope.astype(BF)
            for at in range(0, hidden, wide):
                cut = slice(at, at + wide)
                g_ref[cut, :] = outer(gel[:, cut], dz_ref[...]).astype(BF)

        outs = [
            shaped((width, hidden), BF),
            shaped((all_rows, width), BF),
            shaped((all_rows, hidden), BF),
            shaped((all_rows, hidden), BF),
            shaped((hidden, width), BF),
        ]
        full_up, a2_all, gelled, slope, g_down = call(
            forward, outs, idx, a2_parts + [own_w, up_bias] + got_w + other_w + [dz_all],
            flops=4 * all_rows * width * hidden, mib=54,
        )

        def scatter_ctx(g):
            return lax.psum_scatter(g, "ctx", scatter_dimension=0, tiled=True)

        part_down = scatter_ctx(g_down)

        def backward(i, dz_ref, slope_ref, down, up, du_ref, sum_ref, own, *send):
            total = jnp.zeros((1, hidden), F32)
            for k in range(n_f):
                here = pl.ds(pl.multiple_of((i[FI] ^ k) * rows, rows), rows)
                d_pre = through(dz_ref[here, :], down[...]) * slope_ref[here, :].astype(F32)
                total = total + jnp.sum(d_pre, axis=0, keepdims=True)
                d_hidden = d_pre.astype(BF)
                du_ref[here, :] = d_hidden
                part = through(d_hidden, up[...])
                if k:
                    send[k - 1][...] = part.astype(BF)
                else:
                    own[...] = part
            sum_ref[...] = total

        outs = [
            shaped((all_rows, hidden), BF),
            shaped((1, hidden), F32),
            shaped((rows, width), F32),
        ] + [shaped((rows, width), BF)] * (n_f - 1)
        d_hidden, up_sum, d_own, *sends = call(
            backward, outs, idx, [dz_all, slope, w_down, full_up],
            flops=4 * all_rows * width * hidden, mib=54,
        )
        got_a = send_f(sends)
        g_up = outer(a2_all, d_hidden).astype(BF)

        part_up = scatter_ctx(g_up)

        def second(i, *refs):
            d_ref, mid_ref, small_ref, full, own, refs = (*refs[:5], refs[5:])
            got, refs = refs[: n_f - 1], refs[n_f - 1 :]
            dmid_ref, dy_ref, sums, send = refs[0], refs[1], refs[2], refs[3:]
            d_a = own[...]
            for g in got:
                d_a = d_a + g[...].astype(F32)
            normed, inv = normalize(mid_ref[...])
            d_res = d_ref[...]
            d_mid = d_res + norm_back(d_a * small_ref[1:2, :], normed, inv)
            dmid_ref[...] = d_mid
            dy = d_mid.astype(BF)
            dy_ref[...] = dy
            for m in range(n_f):
                at = pl.multiple_of((m ^ i[Z]) * wide, wide)
                send[m][...] = through(dy, full[pl.ds(at, wide), :]).astype(BF)
            sums[...] = jnp.zeros_like(sums)
            sums[1:2, :] = jnp.sum(d_a * normed, axis=0, keepdims=True)
            sums[5:6, :] = jnp.sum(d_mid, axis=0, keepdims=True)
            sums[6:7, :] = jnp.sum(d_a, axis=0, keepdims=True)
            sums[7:8, :] = jnp.sum(d_res, axis=0, keepdims=True)

        outs = [shaped((rows, width), F32), shaped((rows, width), BF), shaped((8, width), F32)]
        outs += [shaped((rows, wide), BF)] * n_f
        d_mid, dy, sums, *sends = call(
            second, outs, idx, [d_result, mid, small, full_out, d_own] + got_a,
            flops=2 * rows * width * width,
        )
        got = [both_to(sends[m], lambda i, f: (2 * f + i % 2, m ^ (i // 2))) for m in range(n_f)]
        got += [ctx_to(g, 1) for g in got]

        def attend_back(i, *refs):
            seq_ref, att_ref, lse_ref, refs = refs[0], refs[1], refs[2], refs[3:]
            got, refs = refs[: 2 * n_f], refs[2 * n_f :]
            sum_ref, refs = refs[0], refs[1:]
            send, (kpos, qpos, d_out, d_query, d_keys, d_values) = refs[:n_ctx], refs[n_ctx:]
            fill_positions(i, kpos, qpos)
            for m in range(n_f):
                for swap in range(2):
                    part = got[swap * n_f + m]
                    block = (2 * (m ^ i[FI]) + (i[CORE] ^ swap)) ^ i[CI]
                    rows_of = jnp.where(i[CORE] == 0, part[:, :pair], part[:, pair:])
                    for j in range(slots):
                        at = place(i, block, j)
                        d_out[pl.ds(at, blk), :] = rows_of[j * blk : (j + 1) * blk, :]
            d_keys[...] = jnp.zeros_like(d_keys)
            d_values[...] = jnp.zeros_like(d_values)

            def step(span, e, _):
                here = pl.ds(pl.multiple_of(e * tall, tall), tall)
                allowed = kpos[:, :span] <= qpos[here, :]
                for h in range(heads):
                    cut = slice(h * hd, (h + 1) * hd)
                    query, d_att = seq_ref[here, cut], d_out[here, cut]
                    keys = seq_ref[:span, pair + h * hd : pair + (h + 1) * hd]
                    values = seq_ref[:span, 2 * pair + h * hd : 2 * pair + (h + 1) * hd]
                    lse = lse_ref[here, h * hd : h * hd + 1]
                    scores = jnp.where(allowed, through(query, keys), -1e30)
                    probs = jnp.exp(scores - lse)
                    delta = jnp.sum(
                        d_att.astype(F32) * att_ref[here, cut].astype(F32), axis=1, keepdims=True
                    )
                    d_scores = (probs * (through(d_att, values) - delta)).astype(BF)
                    d_query[here, cut] = dot(d_scores, keys) * SCALE
                    d_keys[:span, cut] += outer(d_scores, query)
                    d_values[:span, cut] += outer(probs.astype(BF), d_att)
                return 0

            steps = low_rows // tall
            lax.fori_loop(0, steps, functools.partial(step, low_rows), 0)
            lax.fori_loop(steps, 2 * steps, functools.partial(step, length), 0)
            for e in range(n_ctx):
                for j in range(slots):
                    here, to = pl.ds(place(i, e, j), blk), slice(j * blk, (j + 1) * blk)
                    send[e][to, :pair] = d_query[here, :].astype(BF)
                    send[e][to, pair : 2 * pair] = d_keys[here, :].astype(BF)
                    send[e][to, 2 * pair :] = d_values[here, :].astype(BF)
            sum_ref[...] = jnp.zeros_like(sum_ref)
            sum_ref[3:4, :] = jnp.sum(d_query[...], axis=0, keepdims=True)
            sum_ref[4:5, :] = jnp.sum(d_values[...], axis=0, keepdims=True)

        outs = [shaped((8, pair), F32)] + [shaped((rows, 3 * pair), BF)] * n_ctx
        qv_sum, *sends = call(
            attend_back, outs, idx, [seq, att, lse] + got,
            places
            + [
                pltpu.VMEM((length, pair), BF),
                pltpu.VMEM((length, pair), F32),
                pltpu.VMEM((length, pair), F32),
                pltpu.VMEM((length, pair), F32),
            ],
            flops=10 * length * length * pair,
        )
        got = [sends[0]] + [ctx_to(sends[e], e) for e in range(1, n_ctx)]

        n_all_dev = n_ctx * n_f
        per = width // n_all_dev

        def grad_out(i, dy_ref, *refs):
            o_refs, (away, keep, held) = refs[: 2 * n_f], refs[2 * n_f :]
            for m in range(n_f):
                for core in range(2):
                    at = pl.multiple_of((2 * (m ^ i[Z]) + core) * pair, pair)
                    held[pl.ds(at, pair), :] = outer(o_part(i, o_refs, core, m), dy_ref[...])
            for b in range(n_z):
                for f in range(n_f):
                    at = (2 * b + i[CORE]) * n_f * per + f * per
                    keep[f, b * per : (b + 1) * per, :] = held[pl.ds(at, per), :]
                    at = (2 * b + 1 - i[CORE]) * n_f * per + f * per
                    away[f, b * per : (b + 1) * per, :] = held[pl.ds(at, per), :].astype(BF)

        dims = (n_f, n_z * per, width)
        away, out_keep = call(
            grad_out, [shaped(dims, BF), shaped(dims, F32)], idx, [dy] + o_parts,
            [pltpu.VMEM((width, width), F32)], flops=2 * rows * width * width,
        )
        away = ctx_to(away, 1)

        def out_first(i, keep, got, own, *send):
            f = i[FI]
            own[...] = keep[f] + got[f].astype(F32)
            for k in range(1, n_f):
                send[k - 1][...] = (keep[f ^ k] + got[f ^ k].astype(F32)).astype(BF)

        outs = [shaped((n_z * per, width), F32)] + [shaped((n_z * per, width), BF)] * (n_f - 1)
        out_own, *sends = call(out_first, outs, idx, [out_keep, away])
        out_got = send_f(sends)

        def out_second(i, own_ref, *refs):
            got, (own, *send), held = refs[: n_f - 1], refs[n_f - 1 : -1], refs[-1]
            total = own_ref[...]
            for g in got:
                total = total + g[...].astype(F32)
            held[...] = total
            own[...] = held[pl.ds(pl.multiple_of(i[Z] * per, per), per), :]
            for m in range(1, n_z):
                at = pl.ds(pl.multiple_of((i[Z] ^ m) * per, per), per)
                send[m - 1][...] = held[at, :].astype(BF)

        outs = [shaped((per, width), F32)] + [shaped((per, width), BF)] * (n_z - 1)
        out_own, *sends = call(
            out_second, outs, idx, [out_own] + out_got,
            [pltpu.VMEM((n_z * per, width), F32)],
        )
        out_got = [ctx_to(s, 2 * (m + 1)) for m, s in enumerate(sends)]

        def first(i, *refs):
            got, refs = refs[:n_ctx], refs[n_ctx:]
            n_refs, refs = refs[:n_f], refs[n_f:]
            full, sum_in, refs = refs[0], refs[1], refs[2:]
            proj_ref, sums, own, send, held = refs[0], refs[1], refs[2], refs[3:-1], refs[-1]
            for e in range(n_ctx):
                held[e] = got[e][...]
            gain_sum = jnp.zeros((1, width), F32)
            shift_sum = jnp.zeros((1, width), F32)
            for k in range(n_f):
                here = slice(k * rows, (k + 1) * rows)
                for p in range(2):
                    e = 2 * (i[FI] ^ i[Z] ^ k) + (i[CORE] ^ p)
                    for q in range(3):
                        at = q * wide + p * pair
                        proj_ref[here, at : at + pair] = held[e, :, q * pair : (q + 1) * pair]
                part = through(proj_ref[here, :], full[...])
                gain_sum += jnp.sum(part * n_refs[k][...].astype(F32), axis=0, keepdims=True)
                shift_sum += jnp.sum(part, axis=0, keepdims=True)
                if k:
                    send[k - 1][...] = part.astype(BF)
                else:
                    own[...] = part
            sums[...] = sum_in[...]
            sums[0:1, :] = gain_sum
            sums[2:3, :] = shift_sum

        outs = [
            shaped((all_rows, 3 * wide), BF),
            shaped((8, width), F32),
            shaped((rows, width), F32),
        ] + [shaped((rows, width), BF)] * (n_f - 1)
        d_proj, sums, d_own, *sends = call(
            first, outs, idx, got + n_all + [full_qkv, sums],
            [pltpu.VMEM((n_ctx, rows, 3 * pair), BF)],
            flops=6 * all_rows * width * wide, mib=54,
        )
        got_x = send_f(sends)

        block = width // n_ctx
        per_up = hidden // n_ctx

        def pack(i, a_ref, p_ref, sums_ref, up_ref, qv_ref, away, keep, held):
            f, core = i[FI], i[CORE]
            for zz in range(n_z):
                at = slice(2 * zz * block, 2 * (zz + 1) * block)
                held[...] = outer(a_ref[:, at], p_ref[...])
                both = sums_ref[:, at]
                for par, out in ((core, keep), (1 - core, away)):
                    row = pl.ds(pl.multiple_of(par * block, block), block)
                    out[zz, :block, :] = held[row, :].astype(out.dtype)
                    out[zz, block:, :] = jnp.zeros((16, 3 * wide), out.dtype)
                    hit = jnp.logical_and(zz == f, par == core)
                    small = jnp.where(par == 0, both[:, :block], both[:, block:])
                    small = small + jnp.where(hit, qv_ref[...], 0.0)
                    ups = up_ref[:, pl.ds(pl.multiple_of(par * n_f * per_up, n_f * per_up), n_f * per_up)]
                    ups = jnp.where(zz == f, ups, 0.0)
                    out[zz, block : block + 8, :block] = small.astype(out.dtype)
                    for g in range(n_f):
                        out[zz, block + 8 + g : block + 9 + g, :per_up] = ups[
                            :, g * per_up : (g + 1) * per_up
                        ].astype(out.dtype)

        dims = (n_z, block + 16, 3 * wide)
        away, keep = call(
            pack, [shaped(dims, BF), shaped(dims, F32)], idx,
            [a_all, d_proj, sums, up_sum, qv_sum], [pltpu.VMEM((2 * block, 3 * wide), F32)],
            flops=6 * all_rows * width * wide,
        )
        away = ctx_to(away, 1)

        def over_core(i, keep_ref, got, own, *send):
            own[...] = keep_ref[i[Z]] + got[i[Z]].astype(F32)
            for m in range(1, n_z):
                at = i[Z] ^ m
                send[m - 1][...] = (keep_ref[at] + got[at].astype(F32)).astype(BF)

        outs = [shaped(dims[1:], F32)] + [shaped(dims[1:], BF)] * (n_z - 1)
        own, *sends = call(over_core, outs, idx, [keep, away])
        got = [ctx_to(s, 2 * (m + 1)) for m, s in enumerate(sends)]
        low_down = both_to(part_down, lambda i, f: ((f * n_ctx + i) // n_f, (f * n_ctx + i) % n_f))

        def down(i, gel, w_ref, own, *send):
            for k in range(n_f):
                here = pl.ds(pl.multiple_of((i[FI] ^ k) * rows, rows), rows)
                part = dot(gel[here, :], w_ref[...])
                if k:
                    send[k - 1][...] = part.astype(BF)
                else:
                    own[...] = part

        outs = [shaped((rows, width), F32)] + [shaped((rows, width), BF)] * (n_f - 1)
        z_own, *sends = call(down, outs, idx, [gelled, w_down], flops=2 * all_rows * width * hidden)
        z_got = send_f(sends)

        def add_up(i, own, mid_ref, small_ref, o_ref, *refs):
            got, got_o, (out, o_sum) = refs[: n_f - 1], refs[n_f - 1 : -2], refs[-2:]
            total = own[...]
            for g in got:
                total = total + g[...].astype(F32)
            out[...] = total + mid_ref[...] + small_ref[7:8, :]
            total = o_ref[...]
            for g in got_o:
                total = total + g[...].astype(F32)
            o_sum[...] = total

        result, out_out = call(
            add_up, [shaped((rows, width), F32), shaped((per, width), F32)], idx,
            [z_own, mid, small, out_own] + z_got + out_got,
        )

        def input_grad(i, x_ref, dmid_ref, small_ref, low_ref, own, *refs):
            got, (out, wider) = refs[:-2], refs[-2:]
            normed, inv = normalize(x_ref[...])
            d_a = own[...]
            for g in got:
                d_a = d_a + g[...].astype(F32)
            out[...] = dmid_ref[...] + norm_back(d_a * small_ref[0:1, :], normed, inv)
            wider[...] = low_ref[...].astype(F32)

        outs = [shaped((rows, width), F32), shaped(low_down.shape, F32)]
        d_input, out_down = call(input_grad, outs, idx, [x, d_mid, small, low_down, d_own] + got_x)

        def over_z(i, *refs):
            own_ref, got, up_ref, refs = refs[0], refs[1:n_z], refs[n_z], refs[n_z + 1 :]
            own, send, (held, held_up) = refs[0], refs[1:-2], refs[-2:]
            total = own_ref[...]
            for g in got:
                total = total + g[...].astype(F32)
            held[...] = total
            held_up[...] = up_ref[...].astype(F32)
            for k in range(n_f):
                at = pl.ds(pl.multiple_of((i[FI] ^ k) * per, per), per)
                out = send[k - 1] if k else own
                out[:per, : 3 * wide] = held[at, : 3 * wide].astype(out.dtype)
                out[:per, 3 * wide :] = held_up[at, :].astype(out.dtype)
                out[per:, :] = jnp.zeros((16, 3 * wide + hidden), out.dtype)
                out[per:, : 3 * wide] = held[block:, : 3 * wide].astype(out.dtype)

        dims = (per + 16, 3 * wide + hidden)
        outs = [shaped(dims, F32)] + [shaped(dims, BF)] * (n_f - 1)
        own, *sends = call(
            over_z, outs, idx, [own] + got + [part_up],
            [pltpu.VMEM((block + 16, 3 * wide), F32), pltpu.VMEM((block, hidden), F32)],
            mib=54,
        )
        got = send_f(sends)

        def last(i, own_ref, *refs):
            got, (out, up, small_ref, bias_ref) = refs[: n_f - 1], refs[n_f - 1 :]
            total = own_ref[per:, :block]
            for k in range(n_f):
                src = got[k - 1] if k else own_ref
                for q in range(3):
                    at = pl.ds(pl.multiple_of(q * width + (i[FI] ^ k) * wide, wide), wide)
                    out[:, at] = src[:per, q * wide : (q + 1) * wide].astype(F32)
                at = pl.ds(pl.multiple_of((i[FI] ^ k) * hidden, hidden), hidden)
                up[:, at] = src[:per, 3 * wide :].astype(F32)
                if k:
                    total = total + src[per:, :block].astype(F32)
            share, ups = total[:8, :per], total[8:9, :per_up]
            for g in range(1, n_f):
                share = jnp.where(i[FI] == g, total[:8, g * per : (g + 1) * per], share)
                ups = jnp.where(i[FI] == g, total[8 + g : 9 + g, :per_up], ups)
            small_ref[...] = share
            bias_ref[...] = ups

        outs = [shaped((per, 3 * width), F32), shaped((per, n_f * hidden), F32)]
        outs += [shaped((8, per), F32), shaped((1, per_up), F32)]
        out_qkv, out_up, out_small, out_upb = call(last, outs, idx, [own] + got)

        shape = (seqs, slots, blk, width)
        return (
            result.reshape(shape),
            d_input.reshape(shape),
            out_qkv[None],
            out_out[None],
            out_up[None],
            out_down[None],
            out_small[:2][None],
            out_small[2:][None],
            out_upb.reshape(1, -1),
        )

    return layer


def solution(mesh):
    return jax.shard_map(
        build(mesh),
        mesh=mesh,
        in_specs=(
            P("fsdp", "ctx", None, None),
            P(),
            P(None, "fsdp", None),
            P(None, "fsdp", None),
            P(None, "fsdp", None),
            P(None, "fsdp", None),
            P(None, None, "fsdp"),
            P(None, None, "fsdp"),
            P(None, "fsdp"),
            P("fsdp", "ctx", None, None),
        ),
        out_specs=(
            P("fsdp", "ctx", None, None),
            P("fsdp", "ctx", None, None),
            P(None, ("ctx", "fsdp"), None),
            P(None, ("ctx", "fsdp"), None),
            P(None, ("ctx", "fsdp"), None),
            P(None, ("ctx", "fsdp"), None),
            P(None, None, ("ctx", "fsdp")),
            P(None, None, ("ctx", "fsdp")),
            P(None, ("ctx", "fsdp")),
        ),
        check_vma=False,
    )
```
